32 devices in a mesh: groups: 2 (over x), ctx: 4 (over y, core), head: 4 (over z).
Axes of the slice: x: 2, y: 2, z: 4, core: 2. Of those that a mesh axis runs over, the one named last changes fastest.
Arguments:
- hidden: bfloat16 [2, 2048, 4096], P(None, ('groups', 'ctx'), 'head'), parts along dimension 1, may hold values from -40 to 40
- strand_bases: int32 [2048], P(('groups', 'ctx')), parts along dimension 0, may hold values from 0 to 3
- variant_sites: int32 [256], P('groups'), parts along dimension 0, may hold values from 0 to 1023, as said below
- base_shift: int32 [256], P('groups'), parts along dimension 0, may hold values from 1 to 3
- base_embed: bfloat16 [4, 4096], replicated, may hold values from -6 to 6
- query_weight: bfloat16 [4096, 2048], P(None, 'head')
- key_weight: bfloat16 [4096, 2048], P(None, 'head')
- value_weight: bfloat16 [4096, 2048], P(None, 'head'), may hold values from -0.09375 to 0.09375
- out_weight: bfloat16 [2048, 4096], P('head'), may hold values from -4 to 4
Outputs:
- mixed: bfloat16 [2048, 4096], P(('groups', 'ctx'), 'head'), parts along dimension 0
The draws below stay inside these ranges and needn't reach their ends.
There are 2 independent parts, one for each index of `groups`. The reference program is written for one: setup_inputs(seed, part) draws one part's arguments, and reference() takes and returns one part's arrays. A program takes and returns all parts, laid end to end along the dimension named above; an argument that names none is the same for every part. Nothing has to cross between parts.
Inputs may be any that keep to these rules, and one draw needn't show every extreme that they name: `variant_sites`: distinct positions; each aligned block of 256 positions holds at most 64 of them, and some block holds exactly that many.
All inputs are finite; a program needn't handle non-finite values.
Results may differ from the reference program's by a relative error of at most 0.019.
Values may be sent and summed in bfloat16 or wider, within the bound.
A program may use at most 128 MiB of HBM per device.

```python
import math
import jax
import jax.numpy as jnp
from jax import lax

D = 4096
HEAD_DIM = 128
HEADS = 16
ROWS_DEV = 256
VAR_DEV = 32
SEQ_LEN = 1024
VARS = 128


def draw_hidden(key, part):
    base_draw = jax.random.truncated_normal(jax.random.fold_in(key, 41), -6.0, 6.0, (2, SEQ_LEN, D), jnp.float32)
    base_draw = jnp.clip(base_draw, -40.0, 40.0)
    return base_draw.astype(jnp.bfloat16)


def shared_weights(key):
    head_width = HEADS * HEAD_DIM
    shared = jax.random.truncated_normal(jax.random.fold_in(key, 31), -4.0, 4.0, (D, head_width), jnp.float32) / math.sqrt(D)
    private = jax.random.truncated_normal(jax.random.fold_in(key, 32), -4.0, 4.0, (D, head_width), jnp.float32) / math.sqrt(D)
    return (shared, private)


def draw_query_weight(key, part):
    shared, private = shared_weights(key)
    return shared.astype(jnp.bfloat16)


def draw_key_weight(key, part):
    shared, private = shared_weights(key)
    result = private
    return result.astype(jnp.bfloat16)


def draw_variant_sites(key, part):
    block_total = SEQ_LEN // ROWS_DEV
    slot_cap = 2 * VAR_DEV
    key_order = jax.random.fold_in(key, 51)
    key_shift = jax.random.fold_in(key, 52)
    key_rows = jax.random.fold_in(key, 53)
    key_mix = jax.random.fold_in(key, 54)
    block_order = jax.random.permutation(key_order, block_total)
    shifts = jax.random.randint(key_shift, (block_total // 2,), 0, VAR_DEV + 1)
    shifts = shifts.at[0].set(VAR_DEV)
    signed = jnp.concatenate([shifts, -shifts])
    counts = jnp.zeros((block_total,), jnp.int32).at[block_order].set(VAR_DEV + signed)
    row_keys = jax.random.split(key_rows, block_total)
    row_perm = jax.vmap(lambda sub_key: jax.random.permutation(sub_key, ROWS_DEV))(row_keys)[:, :slot_cap]
    positions = (jnp.arange(block_total, dtype=jnp.int32)[:, None] * ROWS_DEV + row_perm).reshape(-1)
    is_valid = (jnp.arange(slot_cap, dtype=jnp.int32)[None, :] < counts[:, None]).reshape(-1)
    ranked = jnp.argsort(jnp.where(is_valid, 0, 1), stable=True)[:VARS]
    chosen = positions[ranked]
    shuffle = jax.random.permutation(key_mix, VARS)
    return chosen[shuffle].astype(jnp.int32)


def touch_ends(values, own_key, low, high):
    index_at = [jax.random.randint(jax.random.fold_in(own_key, axis), (), 0, length) for axis, length in enumerate(values.shape)]
    main_axis = values.shape.index(max(values.shape))
    beside = index_at[:main_axis] + [(index_at[main_axis] + 1) % values.shape[main_axis]] + index_at[main_axis + 1:]
    return values.at[tuple(index_at)].set(low).at[tuple(beside)].set(high)


def shard_levels(own_key, shape, shards, least, top_value):
    def one(axis_at, shards_of):
        draws = jax.random.uniform(jax.random.fold_in(jax.random.fold_in(own_key, 6), axis_at), (shards_of,), jnp.float32, least / len(shards), top_value / len(shards))
        return jnp.repeat(jnp.exp(draws), shape[axis_at] // shards_of).reshape((-1,) + (1,) * (len(shape) - axis_at - 1))

    factor_of = one(*shards[0])
    for cut in shards[1:]:
        factor_of = factor_of * one(*cut)
    return factor_of


def bell_draw(stream_key, shape, deviation, limit, cuts=(), kind=jnp.bfloat16):
    array = deviation * jax.random.normal(stream_key, shape, jnp.float32)
    if cuts:
        array = array * shard_levels(stream_key, shape, cuts, -0.22, 0.18)
    return jnp.clip(array, -limit, limit).astype(kind)


def setup_inputs(seed: int = 0, part: int = 0) -> dict:
    arg_keys = jax.random.split(jax.random.key(seed), 10)
    own_keys = jax.random.split(jax.random.fold_in(arg_keys[9], part), 10)
    hidden = draw_hidden(jax.random.fold_in(jax.random.fold_in(arg_keys[9], part), 71), part)
    strand_bases = touch_ends(jax.random.randint(own_keys[1], (SEQ_LEN,), 0, 4), jax.random.fold_in(own_keys[1], 1), 0, 3).astype(jnp.int32)
    variant_sites = draw_variant_sites(jax.random.fold_in(jax.random.fold_in(arg_keys[9], part), 71), part)
    base_shift = touch_ends(jax.random.randint(own_keys[3], (VARS,), 1, 4), jax.random.fold_in(own_keys[3], 1), 1, 3).astype(jnp.int32)
    base_embed = bell_draw(arg_keys[4], (4, D), 1.0, 6.0)
    query_weight = draw_query_weight(jax.random.fold_in(arg_keys[9], 71), part)
    key_weight = draw_key_weight(jax.random.fold_in(arg_keys[9], 71), part)
    value_weight = bell_draw(arg_keys[7], (D, HEADS * HEAD_DIM), D ** -0.5, 0.09375, ((1, 4),))
    out_weight = bell_draw(arg_keys[8], (HEADS * HEAD_DIM, D), 2 ** -0.5, 4.0, ((0, 4),))
    return dict(hidden=hidden, strand_bases=strand_bases, variant_sites=variant_sites, base_shift=base_shift, base_embed=base_embed, query_weight=query_weight, key_weight=key_weight, value_weight=value_weight, out_weight=out_weight)


ROPE_BASE = 10000.0

def rotate(values, positions):
    half_dim = values.shape[-1] // 2
    freq_table = jnp.power(ROPE_BASE, -jnp.arange(half_dim, dtype=jnp.float32) * 2.0 / values.shape[-1])
    angle_grid = positions[:, None] * freq_table[None, :]
    cos_part = jnp.cos(angle_grid)[:, None, :]
    sin_part = jnp.sin(angle_grid)[:, None, :]
    lower_half = values[..., :half_dim]
    upper_half = values[..., half_dim:]
    return jnp.concatenate([lower_half * cos_part - upper_half * sin_part, upper_half * cos_part + lower_half * sin_part], axis=-1)

def project_rows(inputs, weight, positions, rotated):
    n_rows = inputs.shape[0]
    product = jnp.dot(inputs, weight, preferred_element_type=jnp.float32)
    product = product.reshape(n_rows, -1, HEAD_DIM)
    if rotated:
        product = rotate(product, positions)
    return product.astype(jnp.bfloat16)

def attend(queries, keys_in, values_in, forward):
    window_iota = jnp.arange(SEQ_LEN, dtype=jnp.int32)
    if forward:
        allowed = window_iota[None, :] <= window_iota[:, None]
    else:
        allowed = window_iota[None, :] >= window_iota[:, None]

    def one_head(operands):
        head_query, head_key, head_value = operands
        scores = jnp.dot(head_query, head_key.T, preferred_element_type=jnp.float32) / math.sqrt(HEAD_DIM)
        masked = jnp.where(allowed, scores, -jnp.inf)
        row_max = lax.optimization_barrier(jnp.max(masked, axis=1, keepdims=True))
        weights = jnp.where(allowed, jnp.exp(scores - row_max), 0.0)
        weights = weights / lax.optimization_barrier(jnp.sum(weights, axis=1, keepdims=True))
        return jnp.dot(weights.astype(jnp.bfloat16), head_value, preferred_element_type=jnp.float32)
    return lax.map(one_head, (queries.transpose(1, 0, 2), keys_in.transpose(1, 0, 2), values_in.transpose(1, 0, 2)))

def reference(hidden, strand_bases, variant_sites, base_shift, base_embed, query_weight, key_weight, value_weight, out_weight):
    embed_table = base_embed.astype(jnp.float32)
    old_base = strand_bases[variant_sites]
    new_base = (old_base + base_shift) % 4
    plus_diff = embed_table[new_base] - embed_table[old_base]
    minus_diff = embed_table[3 - new_base] - embed_table[3 - old_base]
    window_pos = jnp.arange(SEQ_LEN, dtype=jnp.float32)
    plus_pos = window_pos
    minus_pos = SEQ_LEN - 1 - window_pos
    plus_rows = (hidden[0][variant_sites].astype(jnp.float32) + plus_diff).astype(jnp.bfloat16)
    minus_rows = (hidden[1][variant_sites].astype(jnp.float32) + minus_diff).astype(jnp.bfloat16)
    mutant_plus = hidden[0].at[variant_sites].set(plus_rows)
    mutant_minus = hidden[1].at[variant_sites].set(minus_rows)
    outcomes = []
    for inputs, positions, forward in ((hidden[0], plus_pos, True), (mutant_plus, plus_pos, True), (hidden[1], minus_pos, False), (mutant_minus, minus_pos, False)):
        queries = project_rows(inputs, query_weight, positions, True)
        keys_out = project_rows(inputs, key_weight, positions, True)
        values_out = project_rows(inputs, value_weight, positions, False)
        outcomes.append(attend(queries, keys_out, values_out, forward))
    combined = 0.5 * (outcomes[0] - outcomes[1] + (outcomes[2] - outcomes[3]))
    combined = combined.transpose(1, 0, 2).reshape(SEQ_LEN, -1).astype(jnp.bfloat16)
    return jnp.dot(combined, out_weight, preferred_element_type=jnp.float32).astype(jnp.bfloat16)
```

```python
import functools
import math

import jax
import jax.numpy as jnp
import numpy as np
from jax import lax
from jax.experimental import pallas as pl
from jax.experimental.pallas import tpu as pltpu
from jax.sharding import PartitionSpec as P

HEAD_DIM = 128
VAR_DEV = 32
ROPE_BASE = 10000.0
NEG_FILL = -1e30
FAR = 1e9
PIECES = 2
MESH = pl.DeviceIdType.MESH
VMEM_LIMIT = 62 * 1024 * 1024


def iota(shape, axis):
    return lax.broadcasted_iota(jnp.int32, shape, axis).astype(jnp.float32)


def center_out(count):
    half = count // 2
    if count % 2:
        return [(half,)] + [(half - k, half + k) for k in range(1, half + 1)]
    return [(half - 1 - k, half + k) for k in range(half)]


def fused_kernel(
    n_groups,
    n_ctx,
    n_head,
    hidden,
    bases_in,
    sites_in,
    shifts_in,
    embed_in,
    freq_in,
    wq,
    wk,
    wv,
    wo_in,
    out,
    xbuf,
    wbuf,
    wo_own,
    wo_far,
    bases,
    sites,
    shifts,
    embed,
    freq,
    stk,
    acc,
    diff,
    sel,
    sel_t,
    has_row,
    kt,
    cos,
    sin,
    qbuf,
    kvbuf,
    m_buf,
    l_buf,
    a_buf,
    part,
    comb,
    mix,
    small_sem,
    own_sem,
    w_sem,
    xs_sem,
    xr_sem,
    ws_sem,
    wr_sem,
    ps_sem,
    pr_sem,
    ks_sem,
    kr_sem,
    cs_sem,
    cr_sem,
):
    g = lax.axis_index("groups")
    me = lax.axis_index("ctx")
    z = lax.axis_index("head")
    rows, feats = hidden.shape[1], hidden.shape[2]
    hw = wq.shape[1]
    heads = hw // HEAD_DIM
    slots = 2 * VAR_DEV
    window = rows * n_ctx
    piece = rows // PIECES
    plane = n_groups * n_ctx
    place = g * n_ctx + me
    log_scale = math.log2(math.e) / math.sqrt(HEAD_DIM)

    barrier = pltpu.get_barrier_semaphore()

    def greet_line(step, carry):
        other = lax.rem(z + step, n_head)
        pl.semaphore_signal(barrier, inc=1, device_id={"head": other}, device_id_type=MESH)
        return carry

    def greet_plane(step, carry):
        other = lax.rem(place + step, plane)
        pl.semaphore_signal(
            barrier,
            inc=1,
            device_id={"groups": other // n_ctx, "ctx": lax.rem(other, n_ctx)},
            device_id_type=MESH,
        )
        return carry

    lax.fori_loop(1, n_head, greet_line, 0)
    lax.fori_loop(1, plane, greet_plane, 0)
    pl.semaphore_wait(barrier, n_head - 1 + plane - 1)

    part_rows, part_cols = hw // n_ctx, feats // n_groups

    def part_span(owner_group, owner_ctx):
        return (
            pl.ds(pl.multiple_of(owner_ctx * part_rows, part_rows), part_rows),
            pl.ds(pl.multiple_of(owner_group * part_cols, part_cols), part_cols),
        )

    def fetch(step):
        other = lax.rem(z + step, n_head)
        span = part_span(g, me)
        first = pl.multiple_of(other * feats + g * part_cols, part_cols)
        return pltpu.make_async_remote_copy(
            src_ref=wo_in.at[span[0], pl.ds(first, part_cols)],
            dst_ref=wo_far.at[n_head - step - 1, span[0], span[1]],
            send_sem=ws_sem.at[n_head - step - 1],
            recv_sem=wr_sem.at[n_head - step - 1],
            device_id={"head": other},
            device_id_type=MESH,
        )

    def share(step):
        other = lax.rem(place + step, plane)
        span = part_span(g, me)
        return pltpu.make_async_remote_copy(
            src_ref=wo_far.at[:, span[0], span[1]],
            dst_ref=wo_far.at[:, span[0], span[1]],
            send_sem=ps_sem.at[step - 1],
            recv_sem=pr_sem.at[step - 1],
            device_id={"groups": other // n_ctx, "ctx": lax.rem(other, n_ctx)},
            device_id_type=MESH,
        )

    def shared_from(step):
        other = lax.rem(place + plane - step, plane)
        span = part_span(other // n_ctx, lax.rem(other, n_ctx))
        return pltpu.make_async_remote_copy(
            src_ref=wo_far.at[:, span[0], span[1]],
            dst_ref=wo_far.at[:, span[0], span[1]],
            send_sem=ps_sem.at[step - 1],
            recv_sem=pr_sem.at[step - 1],
            device_id={"groups": other // n_ctx, "ctx": lax.rem(other, n_ctx)},
            device_id_type=MESH,
        )

    for step in range(1, n_head):
        fetch(step).start()

    def hop(side, strand, shard, part_id, source):
        span = pl.ds(part_id * piece, piece)
        return pltpu.make_async_remote_copy(
            src_ref=source.at[strand, span] if source is hidden else xbuf.at[strand, shard, span],
            dst_ref=xbuf.at[strand, shard, span],
            send_sem=xs_sem.at[side, strand, shard, part_id],
            recv_sem=xr_sem.at[strand, shard, part_id],
            device_id={"head": z - 1 if side == 0 else z + 1},
            device_id_type=MESH,
        )

    def send_own(side, strand):
        for part_id in range(PIECES):
            hop(side, strand, z, part_id, hidden).start()

    @pl.when(z > 0)
    def _():
        send_own(0, 0)

    @pl.when(z < n_head - 1)
    def _():
        send_own(1, 0)

    @pl.when((z > 0) & (z == n_head - 1))
    def _():
        send_own(0, 1)

    @pl.when((z < n_head - 1) & (z == 0))
    def _():
        send_own(1, 1)

    smalls = [
        pltpu.make_async_copy(source, target, small_sem.at[index])
        for index, (source, target) in enumerate(
            (
                (bases_in, bases),
                (sites_in, sites),
                (shifts_in, shifts),
                (embed_in, embed),
                (freq_in, freq),
            )
        )
    ]
    own = [
        pltpu.make_async_copy(hidden.at[strand], xbuf.at[strand, z], own_sem.at[strand])
        for strand in range(2)
    ]
    loads = [
        pltpu.make_async_copy(weight, wbuf.at[index], w_sem.at[index])
        for index, weight in enumerate((wq, wk, wv))
    ]
    load_out = pltpu.make_async_copy(
        wo_in.at[:, pl.ds(pl.multiple_of(z * feats, feats), feats)], wo_own, w_sem.at[3]
    )
    for copy in smalls + own + loads + [load_out]:
        copy.start()
    for copy in smalls:
        copy.wait()

    start = (me * rows).astype(jnp.float32)
    here = me.astype(jnp.float32)
    v_row = sites[...].astype(jnp.float32)
    count = v_row.shape[1]
    v_col = jnp.sum(
        jnp.where(iota((count, count), 0) == iota((count, count), 1), v_row, 0.0),
        axis=1,
        keepdims=True,
    )

    def block_of(positions):
        total = jnp.zeros_like(positions)
        for edge in range(1, n_ctx):
            total = total + jnp.where(positions >= float(edge * rows), 1.0, 0.0)
        return total

    b_row, b_col = block_of(v_row), block_of(v_col)
    same = b_col == b_row
    rank_col = jnp.sum(jnp.where(same & (v_row < v_col), 1.0, 0.0), axis=1, keepdims=True)
    rank_row = jnp.sum(jnp.where(same & (v_col < v_row), 1.0, 0.0), axis=0, keepdims=True)
    slot_col, slot_row = iota((slots, 1), 0), iota((1, slots), 1)
    row_col, row_row = iota((rows, 1), 0), iota((1, rows), 1)

    match = (slot_col == rank_row) & (b_row == here)
    live_col = jnp.max(jnp.where(match, 1.0, 0.0), axis=1, keepdims=True)
    pos_col = jnp.sum(jnp.where(match, v_row, 0.0), axis=1, keepdims=True)
    shift_col = jnp.sum(
        jnp.where(match, shifts[...].astype(jnp.float32), 0.0), axis=1, keepdims=True
    )
    match_t = (rank_col == slot_row) & (b_col == here)
    live_row = jnp.max(jnp.where(match_t, 1.0, 0.0), axis=0, keepdims=True)
    pos_row = jnp.sum(jnp.where(match_t, v_col, 0.0), axis=0, keepdims=True)
    spot_col = jnp.where(live_col > 0.5, pos_col - start, -1.0)
    spot_row = jnp.where(live_row > 0.5, pos_row - start, -1.0)
    picks = spot_col == row_row
    sel[...] = jnp.where(picks, 1.0, 0.0).astype(jnp.bfloat16)
    places = jnp.where(row_col == spot_row, 1.0, 0.0)
    sel_t[...] = places.astype(jnp.bfloat16)
    has_row[...] = jnp.max(places, axis=1, keepdims=True)
    old = jnp.sum(
        jnp.where(picks, bases[...].astype(jnp.float32), 0.0), axis=1, keepdims=True
    )
    new = old + shift_col
    new = jnp.where(new > 3.5, new - 4.0, new)
    for strand in range(2):
        total = jnp.zeros((slots, embed.shape[1]), jnp.float32)
        for code in range(4):
            want = float(code if strand == 0 else 3 - code)
            coef = jnp.where(new == want, 1.0, 0.0) - jnp.where(old == want, 1.0, 0.0)
            coef = jnp.where(live_col > 0.5, coef, 0.0)
            total = total + coef * embed[pl.ds(code, 1), :].astype(jnp.float32)
        diff[strand] = total

    def clock(strand, where):
        return where if strand == 0 else float(window - 1) - where

    for shard in range(n_ctx):
        hit = (rank_col == slot_row) & (b_col == float(shard))
        live = jnp.max(jnp.where(hit, 1.0, 0.0), axis=0, keepdims=True)
        where_slot = jnp.sum(jnp.where(hit, v_col, 0.0), axis=0, keepdims=True)
        where_key = row_row + float(shard * rows)
        changed = jnp.max(jnp.where(v_col == where_key, 1.0, 0.0), axis=0, keepdims=True)
        for strand in range(2):
            kt[strand, shard, :, pl.ds(0, rows)] = jnp.where(
                changed > 0.5, FAR, clock(strand, where_key)
            )
            kt[strand, shard, :, pl.ds(rows, slots)] = jnp.where(
                live > 0.5, clock(strand, where_slot), FAR
            )

    lane = lax.broadcasted_iota(jnp.int32, (1, HEAD_DIM), 1)
    turn = jnp.where(lane < HEAD_DIM // 2, -1.0, 1.0)
    for strand in range(2):
        for span, where in (
            (pl.ds(0, rows), row_col + start),
            (pl.ds(rows, slots), pos_col),
        ):
            angle = clock(strand, where) * freq[...]
            cos[strand, span, :] = jnp.cos(angle)
            sin[strand, span, :] = jnp.sin(angle) * turn

    for copy in own + loads:
        copy.wait()

    shorter = jnp.minimum(z, n_head - 1 - z)
    long_side = jnp.where(z < n_head - 1 - z, 1, -1)

    def shard_of(step):
        paired = jnp.where(step % 2 == 1, (step + 1) // 2, -((step + 1) // 2))
        return z + jnp.where(step <= 2 * shorter, paired, long_side * (step - shorter))

    def project(strand):
        acc[...] = jnp.zeros_like(acc)

        def step_body(step, carry):
            shard = shard_of(step)
            for part_id in range(PIECES):

                @pl.when(shard > z)
                def _():
                    hop(0, strand, shard, part_id, xbuf).wait_recv()

                    @pl.when(z > 0)
                    def _():
                        hop(0, strand, shard, part_id, xbuf).start()

                @pl.when(shard < z)
                def _():
                    hop(1, strand, shard, part_id, xbuf).wait_recv()

                    @pl.when(z < n_head - 1)
                    def _():
                        hop(1, strand, shard, part_id, xbuf).start()

            if strand == 0:

                @pl.when((shard == n_head - 1) & (z < n_head - 1) & (z > 0))
                def _():
                    send_own(0, 1)

                @pl.when((shard == 0) & (z > 0) & (z < n_head - 1))
                def _():
                    send_own(1, 1)

                @pl.when(step == 1)
                def _():
                    for far in range(1, n_head):
                        fetch(far).wait_recv()

                    def spread(other, inner):
                        share(other).start()
                        return inner

                    lax.fori_loop(1, plane, spread, 0)

            block = xbuf[strand, shard]
            stk[pl.ds(0, rows), :] = block
            first = pl.multiple_of(shard * feats, feats)
            picked = jnp.dot(sel[...], block, preferred_element_type=jnp.float32)
            stk[pl.ds(rows, slots), :] = (
                picked + diff[strand, :, pl.ds(first, feats)]
            ).astype(jnp.bfloat16)
            for index in range(3):
                acc[:, pl.ds(index * hw, hw)] += jnp.dot(
                    stk[...],
                    wbuf[index, pl.ds(first, feats), :],
                    preferred_element_type=jnp.float32,
                )
            return carry

        lax.fori_loop(0, n_head, step_body, 0)

    passes_on = (me < n_ctx - 1, me > 0)

    def pass_kv(strand, shard, head):
        return pltpu.make_async_remote_copy(
            src_ref=kvbuf.at[strand, shard, head],
            dst_ref=kvbuf.at[strand, shard, head],
            send_sem=ks_sem.at[strand, shard, head],
            recv_sem=kr_sem.at[strand, shard, head],
            device_id={"ctx": me + 1 if strand == 0 else me - 1},
            device_id_type=MESH,
        )

    def rotated(strand, index, head):
        raw = acc[:, pl.ds(index * hw + head * HEAD_DIM, HEAD_DIM)]
        return (
            raw * cos[strand] + pltpu.roll(raw, HEAD_DIM // 2, 1) * sin[strand]
        ).astype(jnp.bfloat16)

    def finish(strand):
        def send_head(head):
            @pl.when(passes_on[strand])
            def _():
                pass_kv(strand, me, head).start()

        for head in range(heads):
            kvbuf[strand, me, head, :, pl.ds(0, HEAD_DIM)] = rotated(strand, 1, head)
            kvbuf[strand, me, head, :, pl.ds(HEAD_DIM, HEAD_DIM)] = acc[
                :, pl.ds(2 * hw + head * HEAD_DIM, HEAD_DIM)
            ].astype(jnp.bfloat16)
            if head:
                send_head(head - 1)
        for head in range(heads):
            turned = rotated(strand, 0, head)
            base = turned[:rows]
            placed = jnp.dot(sel_t[...], turned[rows:], preferred_element_type=jnp.float32)
            qbuf[0, head] = base
            qbuf[1, head] = jnp.where(
                has_row[...] > 0.5, placed, base.astype(jnp.float32)
            ).astype(jnp.bfloat16)
            if head == 0:
                send_head(heads - 1)

    def comb_hop(side, shard, head):
        cols = pl.ds(pl.multiple_of(head * HEAD_DIM, HEAD_DIM), HEAD_DIM)
        return pltpu.make_async_remote_copy(
            src_ref=comb.at[shard, :, cols],
            dst_ref=comb.at[shard, :, cols],
            send_sem=cs_sem.at[side, shard, head],
            recv_sem=cr_sem.at[shard, head],
            device_id={"head": z - 1 if side == 0 else z + 1},
            device_id_type=MESH,
        )

    def send_comb(head):
        @pl.when(z > 0)
        def _():
            comb_hop(0, z, head).start()

        @pl.when(z < n_head - 1)
        def _():
            comb_hop(1, z, head).start()

    def attend(strand):
        q_time = clock(strand, row_col + start)

        def update(shard, head, first):
            k_times = (clock(strand, row_row + (shard * rows).astype(jnp.float32)), kt[strand, shard])
            spans = (rows, rows + slots)
            for kind in range(2):
                span = pl.ds(0, spans[kind])
                raw = lax.dot_general(
                    qbuf[kind, head],
                    kvbuf[strand, shard, head, span, pl.ds(0, HEAD_DIM)],
                    (((1,), (1,)), ((), ())),
                    preferred_element_type=jnp.float32,
                )
                if first or kind == 1:
                    raw = jnp.where(k_times[kind] <= q_time, raw, NEG_FILL)
                top = jnp.max(raw, axis=1, keepdims=True)
                if not first:
                    before = m_buf[kind]
                    top = jnp.maximum(before, top)
                    fade = jnp.exp2((before - top) * log_scale)
                weights = jnp.exp2((raw - top) * log_scale)
                total = jnp.sum(weights, axis=1, keepdims=True)
                vec = jnp.dot(
                    weights.astype(jnp.bfloat16),
                    kvbuf[strand, shard, head, span, pl.ds(HEAD_DIM, HEAD_DIM)],
                    preferred_element_type=jnp.float32,
                )
                if not first:
                    total = total + fade * l_buf[kind]
                    vec = vec + fade * a_buf[kind]
                m_buf[kind] = top
                l_buf[kind] = total
                a_buf[kind] = vec

        def one_head(head, carry):
            update(me, head, True)

            def arrive(step, inner):
                shard = me - step if strand == 0 else me + step

                @pl.when(shard >= 0 if strand == 0 else shard < n_ctx)
                def _():
                    pass_kv(strand, shard, head).wait_recv()

                    @pl.when(passes_on[strand])
                    def _():
                        pass_kv(strand, shard, head).start()

                    update(shard, head, False)

                return inner

            lax.fori_loop(1, n_ctx, arrive, 0)
            gap = a_buf[0] / l_buf[0] - a_buf[1] / l_buf[1]
            if strand == 0:
                part[head] = gap
            else:
                cols = pl.ds(pl.multiple_of(head * HEAD_DIM, HEAD_DIM), HEAD_DIM)
                comb[z, :, cols] = (0.5 * (part[head] + gap)).astype(jnp.bfloat16)
                send_comb(head)
            return carry

        lax.fori_loop(0, heads, one_head, 0)

    for strand in range(2):
        project(strand)
        finish(strand)
        attend(strand)

    load_out.wait()
    mix[...] = jnp.dot(comb[z], wo_own[...], preferred_element_type=jnp.float32)

    def collect(step, carry):
        shared_from(step).wait_recv()
        return carry

    lax.fori_loop(1, plane, collect, 0)
    for pair in center_out(n_head):
        for head in range(heads):
            for shard in pair:

                @pl.when(z < shard)
                def _():
                    comb_hop(0, shard, head).wait_recv()

                    @pl.when(z > 0)
                    def _():
                        comb_hop(0, shard, head).start()

                @pl.when(z > shard)
                def _():
                    comb_hop(1, shard, head).wait_recv()

                    @pl.when(z < n_head - 1)
                    def _():
                        comb_hop(1, shard, head).start()

        for shard in pair:

            @pl.when(z != shard)
            def _():
                mix[...] += jnp.dot(
                    comb[shard],
                    wo_far[lax.rem(shard - z - 1 + n_head, n_head)],
                    preferred_element_type=jnp.float32,
                )

    out[...] = mix[...].astype(jnp.bfloat16)

    for step in range(1, n_head):
        fetch(step).wait_send()

    def drain_share(step, carry):
        share(step).wait_send()
        return carry

    lax.fori_loop(1, plane, drain_share, 0)

    def drain_line(shard, carry):
        @pl.when((shard >= z) & (z > 0))
        def _():
            for strand in range(2):
                for part_id in range(PIECES):
                    hop(0, strand, shard, part_id, xbuf).wait_send()
            for head in range(heads):
                comb_hop(0, shard, head).wait_send()

        @pl.when((shard <= z) & (z < n_head - 1))
        def _():
            for strand in range(2):
                for part_id in range(PIECES):
                    hop(1, strand, shard, part_id, xbuf).wait_send()
            for head in range(heads):
                comb_hop(1, shard, head).wait_send()

        return carry

    lax.fori_loop(0, n_head, drain_line, 0)

    def drain_ctx(shard, carry):
        for strand in range(2):

            @pl.when(passes_on[strand] & (shard <= me if strand == 0 else shard >= me))
            def _():
                for head in range(heads):
                    pass_kv(strand, shard, head).wait_send()

        return carry

    lax.fori_loop(0, n_ctx, drain_ctx, 0)


def anywhere():
    return pl.BlockSpec(memory_space=pl.ANY)


def shards(
    hidden,
    strand_bases,
    variant_sites,
    base_shift,
    base_embed,
    query_weight,
    key_weight,
    value_weight,
    out_weight,
):
    rows, feats = hidden.shape[1], hidden.shape[2]
    n_groups = lax.axis_size("groups")
    n_ctx = lax.axis_size("ctx")
    n_head = lax.axis_size("head")
    slots = 2 * VAR_DEV
    wide = rows + slots
    hw = query_weight.shape[1]
    heads = hw // HEAD_DIM
    width = query_weight.shape[0]
    count = variant_sites.shape[0]
    plane = n_groups * n_ctx

    half = HEAD_DIM // 2
    freq = np.power(np.float32(ROPE_BASE), -np.arange(half, dtype=np.float32) * 2.0 / HEAD_DIM)
    freq = np.concatenate([freq, freq]).astype(np.float32)[None, :]

    f32, bf16, i32 = jnp.float32, jnp.bfloat16, jnp.int32
    dma = pltpu.SemaphoreType.DMA
    return pl.pallas_call(
        functools.partial(fused_kernel, n_groups, n_ctx, n_head),
        out_shape=jax.ShapeDtypeStruct((rows, feats), bf16),
        in_specs=[anywhere()] * 10,
        out_specs=pl.BlockSpec(memory_space=pltpu.VMEM),
        scratch_shapes=[
            pltpu.VMEM((2, n_head, rows, feats), bf16),
            pltpu.VMEM((3, width, hw), bf16),
            pltpu.VMEM((hw, feats), bf16),
            pltpu.VMEM((max(n_head - 1, 1), hw, feats), bf16),
            pltpu.VMEM((1, rows), i32),
            pltpu.VMEM((1, count), i32),
            pltpu.VMEM((1, count), i32),
            pltpu.VMEM((4, width), bf16),
            pltpu.VMEM((1, HEAD_DIM), f32),
            pltpu.VMEM((wide, feats), bf16),
            pltpu.VMEM((wide, 3 * hw), f32),
            pltpu.VMEM((2, slots, width), f32),
            pltpu.VMEM((slots, rows), bf16),
            pltpu.VMEM((rows, slots), bf16),
            pltpu.VMEM((rows, 1), f32),
            pltpu.VMEM((2, n_ctx, 1, wide), f32),
            pltpu.VMEM((2, wide, HEAD_DIM), f32),
            pltpu.VMEM((2, wide, HEAD_DIM), f32),
            pltpu.VMEM((2, heads, rows, HEAD_DIM), bf16),
            pltpu.VMEM((2, n_ctx, heads, wide, 2 * HEAD_DIM), bf16),
            pltpu.VMEM((2, rows, 1), f32),
            pltpu.VMEM((2, rows, 1), f32),
            pltpu.VMEM((2, rows, HEAD_DIM), f32),
            pltpu.VMEM((heads, rows, HEAD_DIM), f32),
            pltpu.VMEM((n_head, rows, hw), bf16),
            pltpu.VMEM((rows, feats), f32),
            dma((5,)),
            dma((2,)),
            dma((4,)),
            dma((2, 2, n_head, PIECES)),
            dma((2, n_head, PIECES)),
            dma((max(n_head - 1, 1),)),
            dma((max(n_head - 1, 1),)),
            dma((plane,)),
            dma((plane,)),
            dma((2, n_ctx, heads)),
            dma((2, n_ctx, heads)),
            dma((2, n_head, heads)),
            dma((n_head, heads)),
        ],
        compiler_params=pltpu.CompilerParams(
            collective_id=0, has_side_effects=True, vmem_limit_bytes=VMEM_LIMIT
        ),
        name="fused",
    )(
        hidden,
        strand_bases[None, :],
        variant_sites[None, :],
        base_shift[None, :],
        base_embed,
        jnp.asarray(freq),
        query_weight,
        key_weight,
        value_weight,
        out_weight,
    )


def solution(mesh):
    return jax.shard_map(
        shards,
        mesh=mesh,
        in_specs=(
            P(None, ("groups", "ctx"), "head"),
            P(("groups", "ctx")),
            P("groups"),
            P("groups"),
            P(),
            P(None, "head"),
            P(None, "head"),
            P(None, "head"),
            P("head", None),
        ),
        out_specs=P(("groups", "ctx"), "head"),
        check_vma=False,
    )
```

```python
import functools
import math

import jax
import jax.numpy as jnp
import numpy as np
from jax import lax
from jax.experimental import pallas as pl
from jax.experimental.pallas import tpu as pltpu
from jax.sharding import PartitionSpec as P

HEAD_DIM = 128
VAR_DEV = 32
ROPE_BASE = 10000.0
NEG_FILL = -1e30
FAR = 1e9
PIECES = 2
MESH = pl.DeviceIdType.MESH
VMEM_LIMIT = 62 * 1024 * 1024


def iota(shape, axis):
    return lax.broadcasted_iota(jnp.int32, shape, axis).astype(jnp.float32)


def center_out(count):
    half = count // 2
    if count % 2:
        return [(half, half)] + [(half - k, half + k) for k in range(1, half + 1)]
    return [(half - 1 - k, half + k) for k in range(half)]


def fused_kernel(
    n_groups,
    n_ctx,
    n_head,
    hidden,
    bases_in,
    sites_in,
    shifts_in,
    embed_in,
    freq_in,
    wq,
    wk,
    wv,
    wo_in,
    out,
    xbuf,
    wbuf,
    wo_own,
    wo_far,
    bases,
    sites,
    shifts,
    embed,
    freq,
    stk,
    acc,
    diff,
    sel,
    sel_t,
    has_row,
    kt,
    cos,
    sin,
    qbuf,
    kvbuf,
    m_buf,
    l_buf,
    a_buf,
    part,
    comb,
    mix,
    small_sem,
    own_sem,
    w_sem,
    xs_sem,
    xr_sem,
    ws_sem,
    wr_sem,
    ps_sem,
    pr_sem,
    ks_sem,
    kr_sem,
    cs_sem,
    cr_sem,
):
    g = lax.axis_index("groups")
    me = lax.axis_index("ctx")
    z = lax.axis_index("head")
    rows, feats = hidden.shape[1], hidden.shape[2]
    hw = wq.shape[1]
    heads = hw // HEAD_DIM
    slots = 2 * VAR_DEV
    window = rows * n_ctx
    piece = rows // PIECES
    plane = n_groups * n_ctx
    place = g * n_ctx + me
    log_scale = math.log2(math.e) / math.sqrt(HEAD_DIM)

    barrier = pltpu.get_barrier_semaphore()

    def greet_line(step, carry):
        other = lax.rem(z + step, n_head)
        pl.semaphore_signal(barrier, inc=1, device_id={"head": other}, device_id_type=MESH)
        return carry

    def greet_plane(step, carry):
        other = lax.rem(place + step, plane)
        pl.semaphore_signal(
            barrier,
            inc=1,
            device_id={"groups": other // n_ctx, "ctx": lax.rem(other, n_ctx)},
            device_id_type=MESH,
        )
        return carry

    lax.fori_loop(1, n_head, greet_line, 0)
    lax.fori_loop(1, plane, greet_plane, 0)
    pl.semaphore_wait(barrier, n_head - 1 + plane - 1)

    part_rows, part_cols = hw // n_ctx, feats // n_groups

    def part_span(owner_group, owner_ctx):
        return (
            pl.ds(pl.multiple_of(owner_ctx * part_rows, part_rows), part_rows),
            pl.ds(pl.multiple_of(owner_group * part_cols, part_cols), part_cols),
        )

    def fetch(step):
        other = lax.rem(z + step, n_head)
        span = part_span(g, me)
        first = pl.multiple_of(other * feats + g * part_cols, part_cols)
        return pltpu.make_async_remote_copy(
            src_ref=wo_in.at[span[0], pl.ds(first, part_cols)],
            dst_ref=wo_far.at[n_head - step - 1, span[0], span[1]],
            send_sem=ws_sem.at[n_head - step - 1],
            recv_sem=wr_sem.at[n_head - step - 1],
            device_id={"head": other},
            device_id_type=MESH,
        )

    def share(step):
        other = lax.rem(place + step, plane)
        span = part_span(g, me)
        return pltpu.make_async_remote_copy(
            src_ref=wo_far.at[:, span[0], span[1]],
            dst_ref=wo_far.at[:, span[0], span[1]],
            send_sem=ps_sem.at[step - 1],
            recv_sem=pr_sem.at[step - 1],
            device_id={"groups": other // n_ctx, "ctx": lax.rem(other, n_ctx)},
            device_id_type=MESH,
        )

    def shared_from(step):
        other = lax.rem(place + plane - step, plane)
        span = part_span(other // n_ctx, lax.rem(other, n_ctx))
        return pltpu.make_async_remote_copy(
            src_ref=wo_far.at[:, span[0], span[1]],
            dst_ref=wo_far.at[:, span[0], span[1]],
            send_sem=ps_sem.at[step - 1],
            recv_sem=pr_sem.at[step - 1],
            device_id={"groups": other // n_ctx, "ctx": lax.rem(other, n_ctx)},
            device_id_type=MESH,
        )

    for step in range(1, n_head):
        fetch(step).start()

    def hop(side, strand, shard, part_id, source):
        span = pl.ds(part_id * piece, piece)
        return pltpu.make_async_remote_copy(
            src_ref=source.at[strand, span] if source is hidden else xbuf.at[strand, shard, span],
            dst_ref=xbuf.at[strand, shard, span],
            send_sem=xs_sem.at[side, strand, shard, part_id],
            recv_sem=xr_sem.at[strand, shard, part_id],
            device_id={"head": z - 1 if side == 0 else z + 1},
            device_id_type=MESH,
        )

    def send_own(side, strand):
        for part_id in range(PIECES):
            hop(side, strand, z, part_id, hidden).start()

    @pl.when(z > 0)
    def _():
        send_own(0, 0)

    @pl.when(z < n_head - 1)
    def _():
        send_own(1, 0)

    @pl.when((z > 0) & (z == n_head - 1))
    def _():
        send_own(0, 1)

    @pl.when((z < n_head - 1) & (z == 0))
    def _():
        send_own(1, 1)

    smalls = [
        pltpu.make_async_copy(source, target, small_sem.at[index])
        for index, (source, target) in enumerate(
            (
                (bases_in, bases),
                (sites_in, sites),
                (shifts_in, shifts),
                (embed_in, embed),
                (freq_in, freq),
            )
        )
    ]
    own = [
        pltpu.make_async_copy(hidden.at[strand], xbuf.at[strand, z], own_sem.at[strand])
        for strand in range(2)
    ]
    loads = [
        pltpu.make_async_copy(weight, wbuf.at[index], w_sem.at[index])
        for index, weight in enumerate((wq, wk, wv))
    ]
    load_out = pltpu.make_async_copy(
        wo_in.at[:, pl.ds(pl.multiple_of(z * feats, feats), feats)], wo_own, w_sem.at[3]
    )
    for copy in smalls + own + loads + [load_out]:
        copy.start()
    for copy in smalls:
        copy.wait()

    start = (me * rows).astype(jnp.float32)
    here = me.astype(jnp.float32)
    v_row = sites[...].astype(jnp.float32)
    count = v_row.shape[1]
    v_col = jnp.sum(
        jnp.where(iota((count, count), 0) == iota((count, count), 1), v_row, 0.0),
        axis=1,
        keepdims=True,
    )

    def block_of(positions):
        total = jnp.zeros_like(positions)
        for edge in range(1, n_ctx):
            total = total + jnp.where(positions >= float(edge * rows), 1.0, 0.0)
        return total

    b_row, b_col = block_of(v_row), block_of(v_col)
    same = b_col == b_row
    rank_col = jnp.sum(jnp.where(same & (v_row < v_col), 1.0, 0.0), axis=1, keepdims=True)
    rank_row = jnp.sum(jnp.where(same & (v_col < v_row), 1.0, 0.0), axis=0, keepdims=True)
    slot_col, slot_row = iota((slots, 1), 0), iota((1, slots), 1)
    row_col, row_row = iota((rows, 1), 0), iota((1, rows), 1)

    match = (slot_col == rank_row) & (b_row == here)
    live_col = jnp.max(jnp.where(match, 1.0, 0.0), axis=1, keepdims=True)
    pos_col = jnp.sum(jnp.where(match, v_row, 0.0), axis=1, keepdims=True)
    shift_col = jnp.sum(
        jnp.where(match, shifts[...].astype(jnp.float32), 0.0), axis=1, keepdims=True
    )
    match_t = (rank_col == slot_row) & (b_col == here)
    live_row = jnp.max(jnp.where(match_t, 1.0, 0.0), axis=0, keepdims=True)
    pos_row = jnp.sum(jnp.where(match_t, v_col, 0.0), axis=0, keepdims=True)
    spot_col = jnp.where(live_col > 0.5, pos_col - start, -1.0)
    spot_row = jnp.where(live_row > 0.5, pos_row - start, -1.0)
    picks = spot_col == row_row
    sel[...] = jnp.where(picks, 1.0, 0.0).astype(jnp.bfloat16)
    places = jnp.where(row_col == spot_row, 1.0, 0.0)
    sel_t[...] = places.astype(jnp.bfloat16)
    has_row[...] = jnp.max(places, axis=1, keepdims=True)
    old = jnp.sum(
        jnp.where(picks, bases[...].astype(jnp.float32), 0.0), axis=1, keepdims=True
    )
    new = old + shift_col
    new = jnp.where(new > 3.5, new - 4.0, new)
    for strand in range(2):
        total = jnp.zeros((slots, embed.shape[1]), jnp.float32)
        for code in range(4):
            want = float(code if strand == 0 else 3 - code)
            coef = jnp.where(new == want, 1.0, 0.0) - jnp.where(old == want, 1.0, 0.0)
            coef = jnp.where(live_col > 0.5, coef, 0.0)
            total = total + coef * embed[pl.ds(code, 1), :].astype(jnp.float32)
        diff[strand] = total

    def clock(strand, where):
        return where if strand == 0 else float(window - 1) - where

    for shard in range(n_ctx):
        hit = (rank_col == slot_row) & (b_col == float(shard))
        live = jnp.max(jnp.where(hit, 1.0, 0.0), axis=0, keepdims=True)
        where_slot = jnp.sum(jnp.where(hit, v_col, 0.0), axis=0, keepdims=True)
        where_key = row_row + float(shard * rows)
        changed = jnp.max(jnp.where(v_col == where_key, 1.0, 0.0), axis=0, keepdims=True)
        for strand in range(2):
            kt[strand, shard, :, pl.ds(0, rows)] = jnp.where(
                changed > 0.5, FAR, clock(strand, where_key)
            )
            kt[strand, shard, :, pl.ds(rows, slots)] = jnp.where(
                live > 0.5, clock(strand, where_slot), FAR
            )

    lane = lax.broadcasted_iota(jnp.int32, (1, HEAD_DIM), 1)
    turn = jnp.where(lane < HEAD_DIM // 2, -1.0, 1.0)
    for strand in range(2):
        for span, where in (
            (pl.ds(0, rows), row_col + start),
            (pl.ds(rows, slots), pos_col),
        ):
            angle = clock(strand, where) * freq[...]
            cos[strand, span, :] = jnp.cos(angle)
            sin[strand, span, :] = jnp.sin(angle) * turn

    for copy in own + loads:
        copy.wait()

    shorter = jnp.minimum(z, n_head - 1 - z)
    long_side = jnp.where(z < n_head - 1 - z, 1, -1)

    def shard_of(step):
        paired = jnp.where(step % 2 == 1, (step + 1) // 2, -((step + 1) // 2))
        return z + jnp.where(step <= 2 * shorter, paired, long_side * (step - shorter))

    def project(strand):
        acc[...] = jnp.zeros_like(acc)

        def step_body(step, carry):
            shard = shard_of(step)
            for part_id in range(PIECES):

                @pl.when(shard > z)
                def _():
                    hop(0, strand, shard, part_id, xbuf).wait_recv()

                    @pl.when(z > 0)
                    def _():
                        hop(0, strand, shard, part_id, xbuf).start()

                @pl.when(shard < z)
                def _():
                    hop(1, strand, shard, part_id, xbuf).wait_recv()

                    @pl.when(z < n_head - 1)
                    def _():
                        hop(1, strand, shard, part_id, xbuf).start()

            if strand == 0:

                @pl.when((shard == n_head - 1) & (z < n_head - 1) & (z > 0))
                def _():
                    send_own(0, 1)

                @pl.when((shard == 0) & (z > 0) & (z < n_head - 1))
                def _():
                    send_own(1, 1)

                @pl.when(step == 1)
                def _():
                    for far in range(1, n_head):
                        fetch(far).wait_recv()

                    def spread(other, inner):
                        share(other).start()
                        return inner

                    lax.fori_loop(1, plane, spread, 0)

            block = xbuf[strand, shard]
            stk[pl.ds(0, rows), :] = block
            first = pl.multiple_of(shard * feats, feats)
            picked = jnp.dot(sel[...], block, preferred_element_type=jnp.float32)
            stk[pl.ds(rows, slots), :] = (
                picked + diff[strand, :, pl.ds(first, feats)]
            ).astype(jnp.bfloat16)
            for index in range(3):
                acc[:, pl.ds(index * hw, hw)] += jnp.dot(
                    stk[...],
                    wbuf[index, pl.ds(first, feats), :],
                    preferred_element_type=jnp.float32,
                )
            return carry

        lax.fori_loop(0, n_head, step_body, 0)

    passes_on = (me < n_ctx - 1, me > 0)

    def pass_kv(strand, shard, head):
        return pltpu.make_async_remote_copy(
            src_ref=kvbuf.at[strand, shard, head],
            dst_ref=kvbuf.at[strand, shard, head],
            send_sem=ks_sem.at[strand, shard, head],
            recv_sem=kr_sem.at[strand, shard, head],
            device_id={"ctx": me + 1 if strand == 0 else me - 1},
            device_id_type=MESH,
        )

    def rotated(strand, index, head):
        raw = acc[:, pl.ds(index * hw + head * HEAD_DIM, HEAD_DIM)]
        return (
            raw * cos[strand] + pltpu.roll(raw, HEAD_DIM // 2, 1) * sin[strand]
        ).astype(jnp.bfloat16)

    def finish(strand):
        def send_head(head):
            @pl.when(passes_on[strand])
            def _():
                pass_kv(strand, me, head).start()

        for head in range(heads):
            kvbuf[strand, me, head, :, pl.ds(0, HEAD_DIM)] = rotated(strand, 1, head)
            kvbuf[strand, me, head, :, pl.ds(HEAD_DIM, HEAD_DIM)] = acc[
                :, pl.ds(2 * hw + head * HEAD_DIM, HEAD_DIM)
            ].astype(jnp.bfloat16)
            if head:
                send_head(head - 1)
        for head in range(heads):
            turned = rotated(strand, 0, head)
            base = turned[:rows]
            placed = jnp.dot(sel_t[...], turned[rows:], preferred_element_type=jnp.float32)
            qbuf[strand, 0, head] = base
            qbuf[strand, 1, head] = jnp.where(
                has_row[...] > 0.5, placed, base.astype(jnp.float32)
            ).astype(jnp.bfloat16)
            if head == 0:
                send_head(heads - 1)

    def comb_hop(side, shard, head):
        cols = pl.ds(pl.multiple_of(head * HEAD_DIM, HEAD_DIM), HEAD_DIM)
        return pltpu.make_async_remote_copy(
            src_ref=comb.at[shard, :, cols],
            dst_ref=comb.at[shard, :, cols],
            send_sem=cs_sem.at[side, shard, head],
            recv_sem=cr_sem.at[shard, head],
            device_id={"head": z - 1 if side == 0 else z + 1},
            device_id_type=MESH,
        )

    def send_comb(head):
        @pl.when(z > 0)
        def _():
            comb_hop(0, z, head).start()

        @pl.when(z < n_head - 1)
        def _():
            comb_hop(1, z, head).start()

    def attend(strand):
        q_time = clock(strand, row_col + start)

        def update(shard, head, first):
            k_times = (clock(strand, row_row + (shard * rows).astype(jnp.float32)), kt[strand, shard])
            spans = (rows, rows + slots)
            for kind in range(2):
                span = pl.ds(0, spans[kind])
                raw = lax.dot_general(
                    qbuf[strand, kind, head],
                    kvbuf[strand, shard, head, span, pl.ds(0, HEAD_DIM)],
                    (((1,), (1,)), ((), ())),
                    preferred_element_type=jnp.float32,
                )
                if first or kind == 1:
                    raw = jnp.where(k_times[kind] <= q_time, raw, NEG_FILL)
                top = jnp.max(raw, axis=1, keepdims=True)
                if not first:
                    before = m_buf[kind]
                    top = jnp.maximum(before, top)
                    fade = jnp.exp2((before - top) * log_scale)
                weights = jnp.exp2((raw - top) * log_scale)
                total = jnp.sum(weights, axis=1, keepdims=True)
                vec = jnp.dot(
                    weights.astype(jnp.bfloat16),
                    kvbuf[strand, shard, head, span, pl.ds(HEAD_DIM, HEAD_DIM)],
                    preferred_element_type=jnp.float32,
                )
                if not first:
                    total = total + fade * l_buf[kind]
                    vec = vec + fade * a_buf[kind]
                m_buf[kind] = top
                l_buf[kind] = total
                a_buf[kind] = vec

        def one_head(head, carry):
            update(me, head, True)

            def arrive(step, inner):
                shard = me - step if strand == 0 else me + step

                @pl.when(shard >= 0 if strand == 0 else shard < n_ctx)
                def _():
                    pass_kv(strand, shard, head).wait_recv()

                    @pl.when(passes_on[strand])
                    def _():
                        pass_kv(strand, shard, head).start()

                    update(shard, head, False)

                return inner

            lax.fori_loop(1, n_ctx, arrive, 0)
            gap = a_buf[0] / l_buf[0] - a_buf[1] / l_buf[1]
            if strand == 0:
                part[head] = gap
            else:
                cols = pl.ds(pl.multiple_of(head * HEAD_DIM, HEAD_DIM), HEAD_DIM)
                comb[z, :, cols] = (0.5 * (part[head] + gap)).astype(jnp.bfloat16)
                send_comb(head)
            return carry

        lax.fori_loop(0, heads, one_head, 0)

    at_end = (z == 0) | (z == n_head - 1)
    project(0)
    finish(0)

    @pl.when(at_end)
    def _():
        attend(0)

    project(1)
    finish(1)

    @pl.when(jnp.logical_not(at_end))
    def _():
        attend(0)

    attend(1)

    load_out.wait()
    mix[...] = jnp.dot(comb[z], wo_own[...], preferred_element_type=jnp.float32)

    def collect(step, carry):
        shared_from(step).wait_recv()
        return carry

    lax.fori_loop(1, plane, collect, 0)

    def pass_comb(shard, head):
        @pl.when(z < shard)
        def _():
            comb_hop(0, shard, head).wait_recv()

            @pl.when(z > 0)
            def _():
                comb_hop(0, shard, head).start()

        @pl.when(z > shard)
        def _():
            comb_hop(1, shard, head).wait_recv()

            @pl.when(z < n_head - 1)
            def _():
                comb_hop(1, shard, head).start()

    for low, high in center_out(n_head):
        near = jnp.where(2 * z < n_head, low, high)
        for head in range(heads + 1):
            if head < heads:
                pass_comb(near, head)
            if head and low != high:
                pass_comb(low + high - near, head - 1)

        for shard in (low, high)[: 1 + (low != high)]:

            @pl.when(z != shard)
            def _():
                mix[...] += jnp.dot(
                    comb[shard],
                    wo_far[lax.rem(shard - z - 1 + n_head, n_head)],
                    preferred_element_type=jnp.float32,
                )

    out[...] = mix[...].astype(jnp.bfloat16)

    for step in range(1, n_head):
        fetch(step).wait_send()

    def drain_share(step, carry):
        share(step).wait_send()
        return carry

    lax.fori_loop(1, plane, drain_share, 0)

    def drain_line(shard, carry):
        @pl.when((shard >= z) & (z > 0))
        def _():
            for strand in range(2):
                for part_id in range(PIECES):
                    hop(0, strand, shard, part_id, xbuf).wait_send()
            for head in range(heads):
                comb_hop(0, shard, head).wait_send()

        @pl.when((shard <= z) & (z < n_head - 1))
        def _():
            for strand in range(2):
                for part_id in range(PIECES):
                    hop(1, strand, shard, part_id, xbuf).wait_send()
            for head in range(heads):
                comb_hop(1, shard, head).wait_send()

        return carry

    lax.fori_loop(0, n_head, drain_line, 0)

    def drain_ctx(shard, carry):
        for strand in range(2):

            @pl.when(passes_on[strand] & (shard <= me if strand == 0 else shard >= me))
            def _():
                for head in range(heads):
                    pass_kv(strand, shard, head).wait_send()

        return carry

    lax.fori_loop(0, n_ctx, drain_ctx, 0)


def anywhere():
    return pl.BlockSpec(memory_space=pl.ANY)


def shards(
    hidden,
    strand_bases,
    variant_sites,
    base_shift,
    base_embed,
    query_weight,
    key_weight,
    value_weight,
    out_weight,
):
    rows, feats = hidden.shape[1], hidden.shape[2]
    n_groups = lax.axis_size("groups")
    n_ctx = lax.axis_size("ctx")
    n_head = lax.axis_size("head")
    slots = 2 * VAR_DEV
    wide = rows + slots
    hw = query_weight.shape[1]
    heads = hw // HEAD_DIM
    width = query_weight.shape[0]
    count = variant_sites.shape[0]
    plane = n_groups * n_ctx

    half = HEAD_DIM // 2
    freq = np.power(np.float32(ROPE_BASE), -np.arange(half, dtype=np.float32) * 2.0 / HEAD_DIM)
    freq = np.concatenate([freq, freq]).astype(np.float32)[None, :]

    f32, bf16, i32 = jnp.float32, jnp.bfloat16, jnp.int32
    dma = pltpu.SemaphoreType.DMA
    return pl.pallas_call(
        functools.partial(fused_kernel, n_groups, n_ctx, n_head),
        out_shape=jax.ShapeDtypeStruct((rows, feats), bf16),
        in_specs=[anywhere()] * 10,
        out_specs=pl.BlockSpec(memory_space=pltpu.VMEM),
        scratch_shapes=[
            pltpu.VMEM((2, n_head, rows, feats), bf16),
            pltpu.VMEM((3, width, hw), bf16),
            pltpu.VMEM((hw, feats), bf16),
            pltpu.VMEM((max(n_head - 1, 1), hw, feats), bf16),
            pltpu.VMEM((1, rows), i32),
            pltpu.VMEM((1, count), i32),
            pltpu.VMEM((1, count), i32),
            pltpu.VMEM((4, width), bf16),
            pltpu.VMEM((1, HEAD_DIM), f32),
            pltpu.VMEM((wide, feats), bf16),
            pltpu.VMEM((wide, 3 * hw), f32),
            pltpu.VMEM((2, slots, width), f32),
            pltpu.VMEM((slots, rows), bf16),
            pltpu.VMEM((rows, slots), bf16),
            pltpu.VMEM((rows, 1), f32),
            pltpu.VMEM((2, n_ctx, 1, wide), f32),
            pltpu.VMEM((2, wide, HEAD_DIM), f32),
            pltpu.VMEM((2, wide, HEAD_DIM), f32),
            pltpu.VMEM((2, 2, heads, rows, HEAD_DIM), bf16),
            pltpu.VMEM((2, n_ctx, heads, wide, 2 * HEAD_DIM), bf16),
            pltpu.VMEM((2, rows, 1), f32),
            pltpu.VMEM((2, rows, 1), f32),
            pltpu.VMEM((2, rows, HEAD_DIM), f32),
            pltpu.VMEM((heads, rows, HEAD_DIM), f32),
            pltpu.VMEM((n_head, rows, hw), bf16),
            pltpu.VMEM((rows, feats), f32),
            dma((5,)),
            dma((2,)),
            dma((4,)),
            dma((2, 2, n_head, PIECES)),
            dma((2, n_head, PIECES)),
            dma((max(n_head - 1, 1),)),
            dma((max(n_head - 1, 1),)),
            dma((plane,)),
            dma((plane,)),
            dma((2, n_ctx, heads)),
            dma((2, n_ctx, heads)),
            dma((2, n_head, heads)),
            dma((n_head, heads)),
        ],
        compiler_params=pltpu.CompilerParams(
            collective_id=0, has_side_effects=True, vmem_limit_bytes=VMEM_LIMIT
        ),
        name="fused",
    )(
        hidden,
        strand_bases[None, :],
        variant_sites[None, :],
        base_shift[None, :],
        base_embed,
        jnp.asarray(freq),
        query_weight,
        key_weight,
        value_weight,
        out_weight,
    )


def solution(mesh):
    return jax.shard_map(
        shards,
        mesh=mesh,
        in_specs=(
            P(None, ("groups", "ctx"), "head"),
            P(("groups", "ctx")),
            P("groups"),
            P("groups"),
            P(),
            P(None, "head"),
            P(None, "head"),
            P(None, "head"),
            P("head", None),
        ),
        out_specs=P(("groups", "ctx"), "head"),
        check_vma=False,
    )
```

```python
import functools
import math

import jax
import jax.numpy as jnp
import numpy as np
from jax import lax
from jax.experimental import pallas as pl
from jax.experimental.pallas import tpu as pltpu
from jax.sharding import PartitionSpec as P

HEAD_DIM = 128
VAR_DEV = 32
ROPE_BASE = 10000.0
NEG_FILL = -1e30
FAR = 1e9
PIECES = 2
MESH = pl.DeviceIdType.MESH
VMEM_LIMIT = 62 * 1024 * 1024


def iota(shape, axis):
    return lax.broadcasted_iota(jnp.int32, shape, axis).astype(jnp.float32)


def center_out(count):
    half = count // 2
    if count % 2:
        return [(half, half)] + [(half - k, half + k) for k in range(1, half + 1)]
    return [(half - 1 - k, half + k) for k in range(half)]


def fused_kernel(
    n_groups,
    n_ctx,
    n_head,
    hidden,
    bases_in,
    sites_in,
    shifts_in,
    embed_in,
    freq_in,
    wq,
    wk,
    wv,
    wo_in,
    out,
    xbuf,
    wbuf,
    wo_own,
    wo_far,
    bases,
    sites,
    shifts,
    embed,
    freq,
    stk,
    acc,
    diff,
    sel,
    sel_t,
    has_row,
    kt,
    cos,
    sin,
    qbuf,
    kvbuf,
    m_buf,
    l_buf,
    a_buf,
    part,
    comb,
    mix,
    small_sem,
    own_sem,
    w_sem,
    xs_sem,
    xr_sem,
    ws_sem,
    wr_sem,
    ps_sem,
    pr_sem,
    ks_sem,
    kr_sem,
    es_sem,
    er_sem,
    cs_sem,
    cr_sem,
):
    g = lax.axis_index("groups")
    me = lax.axis_index("ctx")
    z = lax.axis_index("head")
    rows, feats = hidden.shape[1], hidden.shape[2]
    hw = wq.shape[1]
    heads = hw // HEAD_DIM
    slots = 2 * VAR_DEV
    wide = rows + slots
    window = rows * n_ctx
    piece = rows // PIECES
    plane = n_groups * n_ctx
    place = g * n_ctx + me
    log_scale = math.log2(math.e) / math.sqrt(HEAD_DIM)

    barrier = pltpu.get_barrier_semaphore()

    def greet_line(step, carry):
        other = lax.rem(z + step, n_head)
        pl.semaphore_signal(barrier, inc=1, device_id={"head": other}, device_id_type=MESH)
        return carry

    def greet_plane(step, carry):
        other = lax.rem(place + step, plane)
        pl.semaphore_signal(
            barrier,
            inc=1,
            device_id={"groups": other // n_ctx, "ctx": lax.rem(other, n_ctx)},
            device_id_type=MESH,
        )
        return carry

    lax.fori_loop(1, n_head, greet_line, 0)
    lax.fori_loop(1, plane, greet_plane, 0)
    pl.semaphore_wait(barrier, n_head - 1 + plane - 1)

    part_rows, part_cols = hw // n_ctx, feats // n_groups

    def part_span(owner_group, owner_ctx):
        return (
            pl.ds(pl.multiple_of(owner_ctx * part_rows, part_rows), part_rows),
            pl.ds(pl.multiple_of(owner_group * part_cols, part_cols), part_cols),
        )

    def fetch(step):
        other = lax.rem(z + step, n_head)
        span = part_span(g, me)
        first = pl.multiple_of(other * feats + g * part_cols, part_cols)
        return pltpu.make_async_remote_copy(
            src_ref=wo_in.at[span[0], pl.ds(first, part_cols)],
            dst_ref=wo_far.at[n_head - step - 1, span[0], span[1]],
            send_sem=ws_sem.at[n_head - step - 1],
            recv_sem=wr_sem.at[n_head - step - 1],
            device_id={"head": other},
            device_id_type=MESH,
        )

    def share(step):
        other = lax.rem(place + step, plane)
        span = part_span(g, me)
        return pltpu.make_async_remote_copy(
            src_ref=wo_far.at[:, span[0], span[1]],
            dst_ref=wo_far.at[:, span[0], span[1]],
            send_sem=ps_sem.at[step - 1],
            recv_sem=pr_sem.at[step - 1],
            device_id={"groups": other // n_ctx, "ctx": lax.rem(other, n_ctx)},
            device_id_type=MESH,
        )

    def shared_from(step):
        other = lax.rem(place + plane - step, plane)
        span = part_span(other // n_ctx, lax.rem(other, n_ctx))
        return pltpu.make_async_remote_copy(
            src_ref=wo_far.at[:, span[0], span[1]],
            dst_ref=wo_far.at[:, span[0], span[1]],
            send_sem=ps_sem.at[step - 1],
            recv_sem=pr_sem.at[step - 1],
            device_id={"groups": other // n_ctx, "ctx": lax.rem(other, n_ctx)},
            device_id_type=MESH,
        )

    for step in range(1, n_head):
        fetch(step).start()

    def hop(side, strand, shard, part_id, source):
        span = pl.ds(part_id * piece, piece)
        return pltpu.make_async_remote_copy(
            src_ref=source.at[strand, span] if source is hidden else xbuf.at[strand, shard, span],
            dst_ref=xbuf.at[strand, shard, span],
            send_sem=xs_sem.at[side, strand, shard, part_id],
            recv_sem=xr_sem.at[strand, shard, part_id],
            device_id={"head": z - 1 if side == 0 else z + 1},
            device_id_type=MESH,
        )

    rounds = ((0, (0, 1)), (1, (0,)), (1, (1,)))

    def send_own(side, turn):
        strand, parts = rounds[turn]
        for part_id in parts:
            hop(side, strand, z, part_id, hidden).start()

    @pl.when(z > 0)
    def _():
        send_own(0, 0)

    @pl.when(z < n_head - 1)
    def _():
        send_own(1, 0)

    @pl.when((z > 0) & (z == n_head - 1))
    def _():
        send_own(0, 1)
        send_own(0, 2)

    @pl.when((z < n_head - 1) & (z == 0))
    def _():
        send_own(1, 1)
        send_own(1, 2)

    smalls = [
        pltpu.make_async_copy(source, target, small_sem.at[index])
        for index, (source, target) in enumerate(
            (
                (bases_in, bases),
                (sites_in, sites),
                (shifts_in, shifts),
                (embed_in, embed),
                (freq_in, freq),
            )
        )
    ]
    own = [
        pltpu.make_async_copy(hidden.at[strand], xbuf.at[strand, z], own_sem.at[strand])
        for strand in range(2)
    ]
    loads = [
        pltpu.make_async_copy(weight, wbuf.at[index], w_sem.at[index])
        for index, weight in enumerate((wq, wk, wv))
    ]
    load_out = pltpu.make_async_copy(
        wo_in.at[:, pl.ds(pl.multiple_of(z * feats, feats), feats)], wo_own, w_sem.at[3]
    )
    for copy in smalls + own + loads + [load_out]:
        copy.start()
    for copy in smalls:
        copy.wait()

    start = (me * rows).astype(jnp.float32)
    here = me.astype(jnp.float32)
    v_row = sites[...].astype(jnp.float32)
    count = v_row.shape[1]
    v_col = jnp.sum(
        jnp.where(iota((count, count), 0) == iota((count, count), 1), v_row, 0.0),
        axis=1,
        keepdims=True,
    )

    def block_of(positions):
        total = jnp.zeros_like(positions)
        for edge in range(1, n_ctx):
            total = total + jnp.where(positions >= float(edge * rows), 1.0, 0.0)
        return total

    b_row, b_col = block_of(v_row), block_of(v_col)
    same = b_col == b_row
    rank_col = jnp.sum(jnp.where(same & (v_row < v_col), 1.0, 0.0), axis=1, keepdims=True)
    rank_row = jnp.sum(jnp.where(same & (v_col < v_row), 1.0, 0.0), axis=0, keepdims=True)
    slot_col, slot_row = iota((slots, 1), 0), iota((1, slots), 1)
    row_col, row_row = iota((rows, 1), 0), iota((1, rows), 1)

    match = (slot_col == rank_row) & (b_row == here)
    live_col = jnp.max(jnp.where(match, 1.0, 0.0), axis=1, keepdims=True)
    pos_col = jnp.sum(jnp.where(match, v_row, 0.0), axis=1, keepdims=True)
    shift_col = jnp.sum(
        jnp.where(match, shifts[...].astype(jnp.float32), 0.0), axis=1, keepdims=True
    )
    match_t = (rank_col == slot_row) & (b_col == here)
    live_row = jnp.max(jnp.where(match_t, 1.0, 0.0), axis=0, keepdims=True)
    pos_row = jnp.sum(jnp.where(match_t, v_col, 0.0), axis=0, keepdims=True)
    spot_col = jnp.where(live_col > 0.5, pos_col - start, -1.0)
    spot_row = jnp.where(live_row > 0.5, pos_row - start, -1.0)
    picks = spot_col == row_row
    sel[...] = jnp.where(picks, 1.0, 0.0).astype(jnp.bfloat16)
    places = jnp.where(row_col == spot_row, 1.0, 0.0)
    sel_t[...] = places.astype(jnp.bfloat16)
    has_row[...] = jnp.max(places, axis=1, keepdims=True)
    old = jnp.sum(
        jnp.where(picks, bases[...].astype(jnp.float32), 0.0), axis=1, keepdims=True
    )
    new = old + shift_col
    new = jnp.where(new > 3.5, new - 4.0, new)
    for strand in range(2):
        total = jnp.zeros((slots, embed.shape[1]), jnp.float32)
        for code in range(4):
            want = float(code if strand == 0 else 3 - code)
            coef = jnp.where(new == want, 1.0, 0.0) - jnp.where(old == want, 1.0, 0.0)
            coef = jnp.where(live_col > 0.5, coef, 0.0)
            total = total + coef * embed[pl.ds(code, 1), :].astype(jnp.float32)
        diff[strand] = total

    def clock(strand, where):
        return where if strand == 0 else float(window - 1) - where

    for shard in range(n_ctx):
        hit = (rank_col == slot_row) & (b_col == float(shard))
        live = jnp.max(jnp.where(hit, 1.0, 0.0), axis=0, keepdims=True)
        where_slot = jnp.sum(jnp.where(hit, v_col, 0.0), axis=0, keepdims=True)
        where_key = row_row + float(shard * rows)
        changed = jnp.max(jnp.where(v_col == where_key, 1.0, 0.0), axis=0, keepdims=True)
        for strand in range(2):
            kt[strand, shard, :, pl.ds(0, rows)] = jnp.where(
                changed > 0.5, FAR, clock(strand, where_key)
            )
            kt[strand, shard, :, pl.ds(rows, slots)] = jnp.where(
                live > 0.5, clock(strand, where_slot), FAR
            )

    lane = lax.broadcasted_iota(jnp.int32, (1, HEAD_DIM), 1)
    turn = jnp.where(lane < HEAD_DIM // 2, -1.0, 1.0)
    for strand in range(2):
        for span, where in (
            (pl.ds(0, rows), row_col + start),
            (pl.ds(rows, slots), pos_col),
        ):
            angle = clock(strand, where) * freq[...]
            cos[strand, span, :] = jnp.cos(angle)
            sin[strand, span, :] = jnp.sin(angle) * turn

    for copy in own + loads:
        copy.wait()

    shorter = jnp.minimum(z, n_head - 1 - z)
    long_side = jnp.where(z < n_head - 1 - z, 1, -1)

    def shard_of(step):
        paired = jnp.where(step % 2 == 1, (step + 1) // 2, -((step + 1) // 2))
        return z + jnp.where(step <= 2 * shorter, paired, long_side * (step - shorter))

    def project(turn):
        strand, parts = rounds[turn]
        low, high = parts[0] * piece, (parts[-1] + 1) * piece
        last = high == rows
        span = pl.ds(low, high - low)
        taken = pl.ds(low, (wide if last else high) - low)
        acc[taken, :] = jnp.zeros((taken.size, 3 * hw), jnp.float32)

        def step_body(step, carry):
            shard = shard_of(step)
            for part_id in parts:

                @pl.when(shard > z)
                def _():
                    hop(0, strand, shard, part_id, xbuf).wait_recv()

                    @pl.when(z > 0)
                    def _():
                        hop(0, strand, shard, part_id, xbuf).start()

                @pl.when(shard < z)
                def _():
                    hop(1, strand, shard, part_id, xbuf).wait_recv()

                    @pl.when(z < n_head - 1)
                    def _():
                        hop(1, strand, shard, part_id, xbuf).start()

            if turn < 2:

                @pl.when((shard == n_head - 1) & (z < n_head - 1) & (z > 0))
                def _():
                    send_own(0, turn + 1)

                @pl.when((shard == 0) & (z > 0) & (z < n_head - 1))
                def _():
                    send_own(1, turn + 1)

            if turn == 0:

                @pl.when(step == 1)
                def _():
                    for far in range(1, n_head):
                        fetch(far).wait_recv()

                    def spread(other, inner):
                        share(other).start()
                        return inner

                    lax.fori_loop(1, plane, spread, 0)

            block = xbuf[strand, shard, span, :]
            stk[span, :] = block
            first = pl.multiple_of(shard * feats, feats)
            cols = pl.ds(first, feats)
            mutated = diff[strand, :, cols] + jnp.dot(
                sel[:, span], block, preferred_element_type=jnp.float32
            )
            if last:
                stk[pl.ds(rows, slots), :] = mutated.astype(jnp.bfloat16)
            else:
                diff[strand, :, cols] = mutated
            for index in range(3):
                acc[taken, pl.ds(index * hw, hw)] += jnp.dot(
                    stk[taken, :],
                    wbuf[index, cols, :],
                    preferred_element_type=jnp.float32,
                )
            return carry

        lax.fori_loop(0, n_head, step_body, 0)

    passes_on = (me < n_ctx - 1, me > 0)

    def pass_kv(strand, shard, head):
        span = pl.ds(0, wide) if strand == 0 else pl.ds(piece, wide - piece)
        return pltpu.make_async_remote_copy(
            src_ref=kvbuf.at[strand, shard, head, span],
            dst_ref=kvbuf.at[strand, shard, head, span],
            send_sem=ks_sem.at[strand, shard, head],
            recv_sem=kr_sem.at[strand, shard, head],
            device_id={"ctx": me + 1 if strand == 0 else me - 1},
            device_id_type=MESH,
        )

    def early_kv(shard, step):
        return pltpu.make_async_remote_copy(
            src_ref=kvbuf.at[1, shard, :, pl.ds(0, piece)],
            dst_ref=kvbuf.at[1, shard, :, pl.ds(0, piece)],
            send_sem=es_sem.at[step - 1],
            recv_sem=er_sem.at[step - 1],
            device_id={"ctx": me - step},
            device_id_type=MESH,
        )

    def rotated(strand, index, head, span):
        raw = acc[span, pl.ds(index * hw + head * HEAD_DIM, HEAD_DIM)]
        return (
            raw * cos[strand, span, :] + pltpu.roll(raw, HEAD_DIM // 2, 1) * sin[strand, span, :]
        ).astype(jnp.bfloat16)

    def finish(turn):
        strand, parts = rounds[turn]
        low, high = parts[0] * piece, (parts[-1] + 1) * piece
        last = high == rows
        taken = pl.ds(low, (wide if last else high) - low)

        def send_head(head):
            if last:

                @pl.when(passes_on[strand])
                def _():
                    pass_kv(strand, me, head).start()

        for head in range(heads):
            kvbuf[strand, me, head, taken, pl.ds(0, HEAD_DIM)] = rotated(strand, 1, head, taken)
            kvbuf[strand, me, head, taken, pl.ds(HEAD_DIM, HEAD_DIM)] = acc[
                taken, pl.ds(2 * hw + head * HEAD_DIM, HEAD_DIM)
            ].astype(jnp.bfloat16)
            if head:
                send_head(head - 1)
        for head in range(heads):
            turned = rotated(strand, 0, head, taken)
            qbuf[strand, 0, head, pl.ds(low, high - low), :] = turned[: high - low]
            if last:
                placed = jnp.dot(
                    sel_t[...], turned[high - low :], preferred_element_type=jnp.float32
                )
                qbuf[strand, 1, head] = jnp.where(
                    has_row[...] > 0.5, placed, qbuf[strand, 0, head].astype(jnp.float32)
                ).astype(jnp.bfloat16)
            if head == 0:
                send_head(heads - 1)
        if not last:
            for step in range(1, n_ctx):

                @pl.when(me >= step)
                def _():
                    early_kv(me, step).start()

    def comb_hop(side, shard, head):
        cols = pl.ds(pl.multiple_of(head * HEAD_DIM, HEAD_DIM), HEAD_DIM)
        return pltpu.make_async_remote_copy(
            src_ref=comb.at[shard, :, cols],
            dst_ref=comb.at[shard, :, cols],
            send_sem=cs_sem.at[side, shard, head],
            recv_sem=cr_sem.at[shard, head],
            device_id={"head": z - 1 if side == 0 else z + 1},
            device_id_type=MESH,
        )

    def send_comb(head):
        @pl.when(z > 0)
        def _():
            comb_hop(0, z, head).start()

        @pl.when(z < n_head - 1)
        def _():
            comb_hop(1, z, head).start()

    def attend(strand):
        q_time = clock(strand, row_col + start)

        def update(shard, head, first):
            k_times = (clock(strand, row_row + (shard * rows).astype(jnp.float32)), kt[strand, shard])
            spans = (rows, rows + slots)
            for kind in range(2):
                span = pl.ds(0, spans[kind])
                raw = lax.dot_general(
                    qbuf[strand, kind, head],
                    kvbuf[strand, shard, head, span, pl.ds(0, HEAD_DIM)],
                    (((1,), (1,)), ((), ())),
                    preferred_element_type=jnp.float32,
                )
                if first or kind == 1:
                    raw = jnp.where(k_times[kind] <= q_time, raw, NEG_FILL)
                top = jnp.max(raw, axis=1, keepdims=True)
                if not first:
                    before = m_buf[kind]
                    top = jnp.maximum(before, top)
                    fade = jnp.exp2((before - top) * log_scale)
                weights = jnp.exp2((raw - top) * log_scale)
                total = jnp.sum(weights, axis=1, keepdims=True)
                vec = jnp.dot(
                    weights.astype(jnp.bfloat16),
                    kvbuf[strand, shard, head, span, pl.ds(HEAD_DIM, HEAD_DIM)],
                    preferred_element_type=jnp.float32,
                )
                if not first:
                    total = total + fade * l_buf[kind]
                    vec = vec + fade * a_buf[kind]
                m_buf[kind] = top
                l_buf[kind] = total
                a_buf[kind] = vec

        def one_head(head, carry):
            update(me, head, True)

            def arrive(step, inner):
                shard = me - step if strand == 0 else me + step

                @pl.when(shard >= 0 if strand == 0 else shard < n_ctx)
                def _():
                    if strand == 1:

                        @pl.when(head == 0)
                        def _():
                            early_kv(shard, step).wait_recv()

                    pass_kv(strand, shard, head).wait_recv()

                    @pl.when(passes_on[strand])
                    def _():
                        pass_kv(strand, shard, head).start()

                    update(shard, head, False)

                return inner

            lax.fori_loop(1, n_ctx, arrive, 0)
            gap = a_buf[0] / l_buf[0] - a_buf[1] / l_buf[1]
            if strand == 0:
                part[head] = gap
            else:
                cols = pl.ds(pl.multiple_of(head * HEAD_DIM, HEAD_DIM), HEAD_DIM)
                comb[z, :, cols] = (0.5 * (part[head] + gap)).astype(jnp.bfloat16)
                send_comb(head)
            return carry

        lax.fori_loop(0, heads, one_head, 0)

    at_end = (z == 0) | (z == n_head - 1)
    project(0)
    finish(0)
    project(1)
    finish(1)

    @pl.when(at_end)
    def _():
        attend(0)

    project(2)
    finish(2)

    @pl.when(jnp.logical_not(at_end))
    def _():
        attend(0)

    attend(1)

    load_out.wait()
    mix[...] = jnp.dot(comb[z], wo_own[...], preferred_element_type=jnp.float32)

    def collect(step, carry):
        shared_from(step).wait_recv()
        return carry

    lax.fori_loop(1, plane, collect, 0)

    def pass_comb(shard, head):
        @pl.when(z < shard)
        def _():
            comb_hop(0, shard, head).wait_recv()

            @pl.when(z > 0)
            def _():
                comb_hop(0, shard, head).start()

        @pl.when(z > shard)
        def _():
            comb_hop(1, shard, head).wait_recv()

            @pl.when(z < n_head - 1)
            def _():
                comb_hop(1, shard, head).start()

    for low, high in center_out(n_head):
        near = jnp.where(2 * z < n_head, low, high)
        for head in range(heads + 1):
            if head < heads:
                pass_comb(near, head)
            if head and low != high:
                pass_comb(low + high - near, head - 1)

        for shard in (low, high)[: 1 + (low != high)]:

            @pl.when(z != shard)
            def _():
                mix[...] += jnp.dot(
                    comb[shard],
                    wo_far[lax.rem(shard - z - 1 + n_head, n_head)],
                    preferred_element_type=jnp.float32,
                )

    out[...] = mix[...].astype(jnp.bfloat16)

    for step in range(1, n_head):
        fetch(step).wait_send()

    def drain_share(step, carry):
        share(step).wait_send()
        return carry

    lax.fori_loop(1, plane, drain_share, 0)

    def drain_line(shard, carry):
        @pl.when((shard >= z) & (z > 0))
        def _():
            for strand in range(2):
                for part_id in range(PIECES):
                    hop(0, strand, shard, part_id, xbuf).wait_send()
            for head in range(heads):
                comb_hop(0, shard, head).wait_send()

        @pl.when((shard <= z) & (z < n_head - 1))
        def _():
            for strand in range(2):
                for part_id in range(PIECES):
                    hop(1, strand, shard, part_id, xbuf).wait_send()
            for head in range(heads):
                comb_hop(1, shard, head).wait_send()

        return carry

    lax.fori_loop(0, n_head, drain_line, 0)

    def drain_ctx(shard, carry):
        for strand in range(2):

            @pl.when(passes_on[strand] & (shard <= me if strand == 0 else shard >= me))
            def _():
                for head in range(heads):
                    pass_kv(strand, shard, head).wait_send()

        return carry

    lax.fori_loop(0, n_ctx, drain_ctx, 0)
    for step in range(1, n_ctx):

        @pl.when(me >= step)
        def _():
            early_kv(me, step).wait_send()


def anywhere():
    return pl.BlockSpec(memory_space=pl.ANY)


def shards(
    hidden,
    strand_bases,
    variant_sites,
    base_shift,
    base_embed,
    query_weight,
    key_weight,
    value_weight,
    out_weight,
):
    rows, feats = hidden.shape[1], hidden.shape[2]
    n_groups = lax.axis_size("groups")
    n_ctx = lax.axis_size("ctx")
    n_head = lax.axis_size("head")
    slots = 2 * VAR_DEV
    wide = rows + slots
    hw = query_weight.shape[1]
    heads = hw // HEAD_DIM
    width = query_weight.shape[0]
    count = variant_sites.shape[0]
    plane = n_groups * n_ctx

    half = HEAD_DIM // 2
    freq = np.power(np.float32(ROPE_BASE), -np.arange(half, dtype=np.float32) * 2.0 / HEAD_DIM)
    freq = np.concatenate([freq, freq]).astype(np.float32)[None, :]

    f32, bf16, i32 = jnp.float32, jnp.bfloat16, jnp.int32
    dma = pltpu.SemaphoreType.DMA
    return pl.pallas_call(
        functools.partial(fused_kernel, n_groups, n_ctx, n_head),
        out_shape=jax.ShapeDtypeStruct((rows, feats), bf16),
        in_specs=[anywhere()] * 10,
        out_specs=pl.BlockSpec(memory_space=pltpu.VMEM),
        scratch_shapes=[
            pltpu.VMEM((2, n_head, rows, feats), bf16),
            pltpu.VMEM((3, width, hw), bf16),
            pltpu.VMEM((hw, feats), bf16),
            pltpu.VMEM((max(n_head - 1, 1), hw, feats), bf16),
            pltpu.VMEM((1, rows), i32),
            pltpu.VMEM((1, count), i32),
            pltpu.VMEM((1, count), i32),
            pltpu.VMEM((4, width), bf16),
            pltpu.VMEM((1, HEAD_DIM), f32),
            pltpu.VMEM((wide, feats), bf16),
            pltpu.VMEM((wide, 3 * hw), f32),
            pltpu.VMEM((2, slots, width), f32),
            pltpu.VMEM((slots, rows), bf16),
            pltpu.VMEM((rows, slots), bf16),
            pltpu.VMEM((rows, 1), f32),
            pltpu.VMEM((2, n_ctx, 1, wide), f32),
            pltpu.VMEM((2, wide, HEAD_DIM), f32),
            pltpu.VMEM((2, wide, HEAD_DIM), f32),
            pltpu.VMEM((2, 2, heads, rows, HEAD_DIM), bf16),
            pltpu.VMEM((2, n_ctx, heads, wide, 2 * HEAD_DIM), bf16),
            pltpu.VMEM((2, rows, 1), f32),
            pltpu.VMEM((2, rows, 1), f32),
            pltpu.VMEM((2, rows, HEAD_DIM), f32),
            pltpu.VMEM((heads, rows, HEAD_DIM), f32),
            pltpu.VMEM((n_head, rows, hw), bf16),
            pltpu.VMEM((rows, feats), f32),
            dma((5,)),
            dma((2,)),
            dma((4,)),
            dma((2, 2, n_head, PIECES)),
            dma((2, n_head, PIECES)),
            dma((max(n_head - 1, 1),)),
            dma((max(n_head - 1, 1),)),
            dma((plane,)),
            dma((plane,)),
            dma((2, n_ctx, heads)),
            dma((2, n_ctx, heads)),
            dma((max(n_ctx - 1, 1),)),
            dma((max(n_ctx - 1, 1),)),
            dma((2, n_head, heads)),
            dma((n_head, heads)),
        ],
        compiler_params=pltpu.CompilerParams(
            collective_id=0, has_side_effects=True, vmem_limit_bytes=VMEM_LIMIT
        ),
        name="fused",
    )(
        hidden,
        strand_bases[None, :],
        variant_sites[None, :],
        base_shift[None, :],
        base_embed,
        jnp.asarray(freq),
        query_weight,
        key_weight,
        value_weight,
        out_weight,
    )


def solution(mesh):
    return jax.shard_map(
        shards,
        mesh=mesh,
        in_specs=(
            P(None, ("groups", "ctx"), "head"),
            P(("groups", "ctx")),
            P("groups"),
            P("groups"),
            P(),
            P(None, "head"),
            P(None, "head"),
            P(None, "head"),
            P("head", None),
        ),
        out_specs=P(("groups", "ctx"), "head"),
        check_vma=False,
    )
```

```python
import functools
import math

import jax
import jax.numpy as jnp
import numpy as np
from jax import lax
from jax.experimental import pallas as pl
from jax.experimental.pallas import tpu as pltpu
from jax.sharding import PartitionSpec as P

HEAD_DIM = 128
VAR_DEV = 32
ROPE_BASE = 10000.0
NEG_FILL = -1e30
FAR = 1e9
PIECES = 2
MESH = pl.DeviceIdType.MESH
VMEM_LIMIT = 62 * 1024 * 1024


def iota(shape, axis):
    return lax.broadcasted_iota(jnp.int32, shape, axis).astype(jnp.float32)


def center_out(count):
    half = count // 2
    if count % 2:
        return [(half, half)] + [(half - k, half + k) for k in range(1, half + 1)]
    return [(half - 1 - k, half + k) for k in range(half)]


def fused_kernel(
    n_groups,
    n_ctx,
    n_head,
    hidden,
    bases_in,
    sites_in,
    shifts_in,
    embed_in,
    freq_in,
    wq,
    wk,
    wv,
    wo_in,
    out,
    xbuf,
    wbuf,
    wo_own,
    wo_far,
    bases,
    sites,
    shifts,
    embed,
    freq,
    stk,
    acc,
    diff,
    sel,
    sel_t,
    has_row,
    kt,
    cos,
    sin,
    qbuf,
    kvbuf,
    m_buf,
    l_buf,
    a_buf,
    part,
    comb,
    mix,
    small_sem,
    own_sem,
    w_sem,
    xs_sem,
    xr_sem,
    ws_sem,
    wr_sem,
    ps_sem,
    pr_sem,
    ks_sem,
    kr_sem,
    es_sem,
    er_sem,
    cs_sem,
    cr_sem,
):
    g = lax.axis_index("groups")
    me = lax.axis_index("ctx")
    z = lax.axis_index("head")
    rows, feats = hidden.shape[1], hidden.shape[2]
    hw = wq.shape[1]
    heads = hw // HEAD_DIM
    slots = 2 * VAR_DEV
    wide = rows + slots
    window = rows * n_ctx
    piece = rows // PIECES
    plane = n_groups * n_ctx
    place = g * n_ctx + me
    log_scale = math.log2(math.e) / math.sqrt(HEAD_DIM)

    barrier = pltpu.get_barrier_semaphore()

    def greet_line(step, carry):
        other = lax.rem(z + step, n_head)
        pl.semaphore_signal(barrier, inc=1, device_id={"head": other}, device_id_type=MESH)
        return carry

    def greet_plane(step, carry):
        other = lax.rem(place + step, plane)
        pl.semaphore_signal(
            barrier,
            inc=1,
            device_id={"groups": other // n_ctx, "ctx": lax.rem(other, n_ctx)},
            device_id_type=MESH,
        )
        return carry

    lax.fori_loop(1, n_head, greet_line, 0)
    lax.fori_loop(1, plane, greet_plane, 0)
    pl.semaphore_wait(barrier, n_head - 1 + plane - 1)

    part_rows, part_cols = hw // n_ctx, feats // n_groups

    def part_span(owner_group, owner_ctx):
        return (
            pl.ds(pl.multiple_of(owner_ctx * part_rows, part_rows), part_rows),
            pl.ds(pl.multiple_of(owner_group * part_cols, part_cols), part_cols),
        )

    def fetch(step):
        other = lax.rem(z + step, n_head)
        span = part_span(g, me)
        first = pl.multiple_of(other * feats + g * part_cols, part_cols)
        return pltpu.make_async_remote_copy(
            src_ref=wo_in.at[span[0], pl.ds(first, part_cols)],
            dst_ref=wo_far.at[n_head - step - 1, span[0], span[1]],
            send_sem=ws_sem.at[n_head - step - 1],
            recv_sem=wr_sem.at[n_head - step - 1],
            device_id={"head": other},
            device_id_type=MESH,
        )

    def share(step):
        other = lax.rem(place + step, plane)
        span = part_span(g, me)
        return pltpu.make_async_remote_copy(
            src_ref=wo_far.at[:, span[0], span[1]],
            dst_ref=wo_far.at[:, span[0], span[1]],
            send_sem=ps_sem.at[step - 1],
            recv_sem=pr_sem.at[step - 1],
            device_id={"groups": other // n_ctx, "ctx": lax.rem(other, n_ctx)},
            device_id_type=MESH,
        )

    def shared_from(step):
        other = lax.rem(place + plane - step, plane)
        span = part_span(other // n_ctx, lax.rem(other, n_ctx))
        return pltpu.make_async_remote_copy(
            src_ref=wo_far.at[:, span[0], span[1]],
            dst_ref=wo_far.at[:, span[0], span[1]],
            send_sem=ps_sem.at[step - 1],
            recv_sem=pr_sem.at[step - 1],
            device_id={"groups": other // n_ctx, "ctx": lax.rem(other, n_ctx)},
            device_id_type=MESH,
        )

    for step in range(1, n_head):
        fetch(step).start()

    def hop(side, strand, shard, part_id, source):
        span = pl.ds(part_id * piece, piece)
        return pltpu.make_async_remote_copy(
            src_ref=source.at[strand, span] if source is hidden else xbuf.at[strand, shard, span],
            dst_ref=xbuf.at[strand, shard, span],
            send_sem=xs_sem.at[side, strand, shard, part_id],
            recv_sem=xr_sem.at[strand, shard, part_id],
            device_id={"head": z - 1 if side == 0 else z + 1},
            device_id_type=MESH,
        )

    rounds = ((0, (0, 1)), (1, (0,)), (1, (1,)))

    def send_own(side, turn):
        strand, parts = rounds[turn]
        for part_id in parts:
            hop(side, strand, z, part_id, hidden).start()

    @pl.when(z > 0)
    def _():
        send_own(0, 0)

    @pl.when(z < n_head - 1)
    def _():
        send_own(1, 0)

    @pl.when((z > 0) & (z == n_head - 1))
    def _():
        send_own(0, 1)
        send_own(0, 2)

    @pl.when((z < n_head - 1) & (z == 0))
    def _():
        send_own(1, 1)
        send_own(1, 2)

    smalls = [
        pltpu.make_async_copy(source, target, small_sem.at[index])
        for index, (source, target) in enumerate(
            (
                (bases_in, bases),
                (sites_in, sites),
                (shifts_in, shifts),
                (embed_in, embed),
                (freq_in, freq),
            )
        )
    ]
    own = [
        pltpu.make_async_copy(hidden.at[strand], xbuf.at[strand, z], own_sem.at[strand])
        for strand in range(2)
    ]
    loads = [
        pltpu.make_async_copy(weight, wbuf.at[index], w_sem.at[index])
        for index, weight in enumerate((wq, wk, wv))
    ]
    load_out = pltpu.make_async_copy(
        wo_in.at[:, pl.ds(pl.multiple_of(z * feats, feats), feats)], wo_own, w_sem.at[3]
    )
    for copy in smalls + own + loads + [load_out]:
        copy.start()
    for copy in smalls:
        copy.wait()

    start = (me * rows).astype(jnp.float32)
    here = me.astype(jnp.float32)
    v_row = sites[...].astype(jnp.float32)
    count = v_row.shape[1]
    v_col = jnp.sum(
        jnp.where(iota((count, count), 0) == iota((count, count), 1), v_row, 0.0),
        axis=1,
        keepdims=True,
    )

    def block_of(positions):
        total = jnp.zeros_like(positions)
        for edge in range(1, n_ctx):
            total = total + jnp.where(positions >= float(edge * rows), 1.0, 0.0)
        return total

    b_row, b_col = block_of(v_row), block_of(v_col)
    same = b_col == b_row
    rank_col = jnp.sum(jnp.where(same & (v_row < v_col), 1.0, 0.0), axis=1, keepdims=True)
    rank_row = jnp.sum(jnp.where(same & (v_col < v_row), 1.0, 0.0), axis=0, keepdims=True)
    slot_col, slot_row = iota((slots, 1), 0), iota((1, slots), 1)
    row_col, row_row = iota((rows, 1), 0), iota((1, rows), 1)

    match = (slot_col == rank_row) & (b_row == here)
    live_col = jnp.max(jnp.where(match, 1.0, 0.0), axis=1, keepdims=True)
    pos_col = jnp.sum(jnp.where(match, v_row, 0.0), axis=1, keepdims=True)
    shift_col = jnp.sum(
        jnp.where(match, shifts[...].astype(jnp.float32), 0.0), axis=1, keepdims=True
    )
    match_t = (rank_col == slot_row) & (b_col == here)
    live_row = jnp.max(jnp.where(match_t, 1.0, 0.0), axis=0, keepdims=True)
    pos_row = jnp.sum(jnp.where(match_t, v_col, 0.0), axis=0, keepdims=True)
    spot_col = jnp.where(live_col > 0.5, pos_col - start, -1.0)
    spot_row = jnp.where(live_row > 0.5, pos_row - start, -1.0)
    picks = spot_col == row_row
    sel[...] = jnp.where(picks, 1.0, 0.0).astype(jnp.bfloat16)
    places = jnp.where(row_col == spot_row, 1.0, 0.0)
    sel_t[...] = places.astype(jnp.bfloat16)
    has_row[...] = jnp.max(places, axis=1, keepdims=True)
    old = jnp.sum(
        jnp.where(picks, bases[...].astype(jnp.float32), 0.0), axis=1, keepdims=True
    )
    new = old + shift_col
    new = jnp.where(new > 3.5, new - 4.0, new)
    for strand in range(2):
        total = jnp.zeros((slots, embed.shape[1]), jnp.float32)
        for code in range(4):
            want = float(code if strand == 0 else 3 - code)
            coef = jnp.where(new == want, 1.0, 0.0) - jnp.where(old == want, 1.0, 0.0)
            coef = jnp.where(live_col > 0.5, coef, 0.0)
            total = total + coef * embed[pl.ds(code, 1), :].astype(jnp.float32)
        diff[strand] = total

    def clock(strand, where):
        return where if strand == 0 else float(window - 1) - where

    for shard in range(n_ctx):
        hit = (rank_col == slot_row) & (b_col == float(shard))
        live = jnp.max(jnp.where(hit, 1.0, 0.0), axis=0, keepdims=True)
        where_slot = jnp.sum(jnp.where(hit, v_col, 0.0), axis=0, keepdims=True)
        where_key = row_row + float(shard * rows)
        changed = jnp.max(jnp.where(v_col == where_key, 1.0, 0.0), axis=0, keepdims=True)
        for strand in range(2):
            kt[strand, shard, :, pl.ds(0, rows)] = jnp.where(
                changed > 0.5, FAR, clock(strand, where_key)
            )
            kt[strand, shard, :, pl.ds(rows, slots)] = jnp.where(
                live > 0.5, clock(strand, where_slot), FAR
            )

    lane = lax.broadcasted_iota(jnp.int32, (1, HEAD_DIM), 1)
    turn = jnp.where(lane < HEAD_DIM // 2, -1.0, 1.0)
    for strand in range(2):
        for span, where in (
            (pl.ds(0, rows), row_col + start),
            (pl.ds(rows, slots), pos_col),
        ):
            angle = clock(strand, where) * freq[...]
            cos[strand, span, :] = jnp.cos(angle)
            sin[strand, span, :] = jnp.sin(angle) * turn

    for copy in own + loads:
        copy.wait()

    shorter = jnp.minimum(z, n_head - 1 - z)
    long_side = jnp.where(z < n_head - 1 - z, 1, -1)

    def shard_of(step):
        paired = jnp.where(step % 2 == 1, (step + 1) // 2, -((step + 1) // 2))
        return z + jnp.where(step <= 2 * shorter, paired, long_side * (step - shorter))

    def project(turn):
        strand, parts = rounds[turn]
        low, high = parts[0] * piece, (parts[-1] + 1) * piece
        last = high == rows
        span = pl.ds(low, high - low)
        taken = pl.ds(low, (wide if last else high) - low)
        acc[taken, :] = jnp.zeros((taken.size, 3 * hw), jnp.float32)

        def step_body(step, carry):
            shard = shard_of(step)
            for part_id in parts:

                @pl.when(shard > z)
                def _():
                    hop(0, strand, shard, part_id, xbuf).wait_recv()

                    @pl.when(z > 0)
                    def _():
                        hop(0, strand, shard, part_id, xbuf).start()

                @pl.when(shard < z)
                def _():
                    hop(1, strand, shard, part_id, xbuf).wait_recv()

                    @pl.when(z < n_head - 1)
                    def _():
                        hop(1, strand, shard, part_id, xbuf).start()

            if turn < 2:

                @pl.when((shard == n_head - 1) & (z < n_head - 1) & (z > 0))
                def _():
                    send_own(0, turn + 1)

                @pl.when((shard == 0) & (z > 0) & (z < n_head - 1))
                def _():
                    send_own(1, turn + 1)

            if turn == 0:

                @pl.when(step == 1)
                def _():
                    for far in range(1, n_head):
                        fetch(far).wait_recv()

                    def spread(other, inner):
                        share(other).start()
                        return inner

                    lax.fori_loop(1, plane, spread, 0)

            block = xbuf[strand, shard, span, :]
            stk[span, :] = block
            first = pl.multiple_of(shard * feats, feats)
            cols = pl.ds(first, feats)
            mutated = diff[strand, :, cols] + jnp.dot(
                sel[:, span], block, preferred_element_type=jnp.float32
            )
            if last:
                stk[pl.ds(rows, slots), :] = mutated.astype(jnp.bfloat16)
            else:
                diff[strand, :, cols] = mutated
            for index in range(3):
                acc[taken, pl.ds(index * hw, hw)] += jnp.dot(
                    stk[taken, :],
                    wbuf[index, cols, :],
                    preferred_element_type=jnp.float32,
                )
            return carry

        lax.fori_loop(0, n_head, step_body, 0)

    passes_on = (me < n_ctx - 1, me > 0)

    def pass_kv(strand, shard, head):
        span = pl.ds(0, wide) if strand == 0 else pl.ds(piece, wide - piece)
        return pltpu.make_async_remote_copy(
            src_ref=kvbuf.at[strand, shard, head, span],
            dst_ref=kvbuf.at[strand, shard, head, span],
            send_sem=ks_sem.at[strand, shard, head],
            recv_sem=kr_sem.at[strand, shard, head],
            device_id={"ctx": me + 1 if strand == 0 else me - 1},
            device_id_type=MESH,
        )

    def early_kv(shard, step):
        return pltpu.make_async_remote_copy(
            src_ref=kvbuf.at[1, shard, :, pl.ds(0, piece)],
            dst_ref=kvbuf.at[1, shard, :, pl.ds(0, piece)],
            send_sem=es_sem.at[step - 1],
            recv_sem=er_sem.at[step - 1],
            device_id={"ctx": me - step},
            device_id_type=MESH,
        )

    def rotated(strand, index, head, span):
        raw = acc[span, pl.ds(index * hw + head * HEAD_DIM, HEAD_DIM)]
        return (
            raw * cos[strand, span, :] + pltpu.roll(raw, HEAD_DIM // 2, 1) * sin[strand, span, :]
        ).astype(jnp.bfloat16)

    def finish(turn):
        strand, parts = rounds[turn]
        low, high = parts[0] * piece, (parts[-1] + 1) * piece
        last = high == rows
        taken = pl.ds(low, (wide if last else high) - low)

        def send_head(head):
            if last:

                @pl.when(passes_on[strand])
                def _():
                    pass_kv(strand, me, head).start()

        for head in range(heads):
            kvbuf[strand, me, head, taken, pl.ds(0, HEAD_DIM)] = rotated(strand, 1, head, taken)
            kvbuf[strand, me, head, taken, pl.ds(HEAD_DIM, HEAD_DIM)] = acc[
                taken, pl.ds(2 * hw + head * HEAD_DIM, HEAD_DIM)
            ].astype(jnp.bfloat16)
            if head:
                send_head(head - 1)
        for head in range(heads):
            turned = rotated(strand, 0, head, taken)
            qbuf[strand, 0, head, pl.ds(low, high - low), :] = turned[: high - low]
            if last:
                placed = jnp.dot(
                    sel_t[...], turned[high - low :], preferred_element_type=jnp.float32
                )
                qbuf[strand, 1, head] = jnp.where(
                    has_row[...] > 0.5, placed, qbuf[strand, 0, head].astype(jnp.float32)
                ).astype(jnp.bfloat16)
            if head == 0:
                send_head(heads - 1)
        if not last:
            for step in range(1, n_ctx):

                @pl.when(me >= step)
                def _():
                    early_kv(me, step).start()

    def comb_hop(side, shard, head):
        cols = pl.ds(pl.multiple_of(head * HEAD_DIM, HEAD_DIM), HEAD_DIM)
        return pltpu.make_async_remote_copy(
            src_ref=comb.at[shard, :, cols],
            dst_ref=comb.at[shard, :, cols],
            send_sem=cs_sem.at[side, shard, head],
            recv_sem=cr_sem.at[shard, head],
            device_id={"head": z - 1 if side == 0 else z + 1},
            device_id_type=MESH,
        )

    def send_comb(head):
        @pl.when(z > 0)
        def _():
            comb_hop(0, z, head).start()

        @pl.when(z < n_head - 1)
        def _():
            comb_hop(1, z, head).start()

    def attend(strand):
        q_time = clock(strand, row_col + start)

        def update(shard, head, first):
            k_times = (clock(strand, row_row + (shard * rows).astype(jnp.float32)), kt[strand, shard])
            spans = (rows, rows + slots)
            raws = [
                lax.dot_general(
                    qbuf[strand, kind, head],
                    kvbuf[strand, shard, head, pl.ds(0, spans[kind]), pl.ds(0, HEAD_DIM)],
                    (((1,), (1,)), ((), ())),
                    preferred_element_type=jnp.float32,
                )
                for kind in range(2)
            ]
            weighted = []
            for kind in range(2):
                raw = raws[kind]
                if first:
                    raw = jnp.where(k_times[kind] <= q_time, raw, NEG_FILL)
                elif kind:
                    raw = jnp.where(k_times[kind] < 0.5 * FAR, raw, NEG_FILL)
                top = jnp.max(raw, axis=1, keepdims=True)
                fade = None
                if not first:
                    before = m_buf[kind]
                    top = jnp.maximum(before, top)
                    fade = jnp.exp2((before - top) * log_scale)
                weights = jnp.exp2((raw - top) * log_scale)
                total = jnp.sum(weights, axis=1, keepdims=True)
                m_buf[kind] = top
                l_buf[kind] = total if first else total + fade * l_buf[kind]
                weighted.append((weights.astype(jnp.bfloat16), fade))
            for kind in range(2):
                weights, fade = weighted[kind]
                vec = jnp.dot(
                    weights,
                    kvbuf[strand, shard, head, pl.ds(0, spans[kind]), pl.ds(HEAD_DIM, HEAD_DIM)],
                    preferred_element_type=jnp.float32,
                )
                a_buf[kind] = vec if first else vec + fade * a_buf[kind]

        def one_head(head, carry):
            update(me, head, True)

            def arrive(step, inner):
                shard = me - step if strand == 0 else me + step

                @pl.when(shard >= 0 if strand == 0 else shard < n_ctx)
                def _():
                    if strand == 1:

                        @pl.when(head == 0)
                        def _():
                            early_kv(shard, step).wait_recv()

                    pass_kv(strand, shard, head).wait_recv()

                    @pl.when(passes_on[strand])
                    def _():
                        pass_kv(strand, shard, head).start()

                    update(shard, head, False)

                return inner

            lax.fori_loop(1, n_ctx, arrive, 0)
            gap = a_buf[0] / l_buf[0] - a_buf[1] / l_buf[1]
            if strand == 0:
                part[head] = gap
            else:
                cols = pl.ds(pl.multiple_of(head * HEAD_DIM, HEAD_DIM), HEAD_DIM)
                comb[z, :, cols] = (0.5 * (part[head] + gap)).astype(jnp.bfloat16)
                send_comb(head)
            return carry

        lax.fori_loop(0, heads, one_head, 0)

    at_end = (z == 0) | (z == n_head - 1)
    project(0)
    finish(0)
    project(1)
    finish(1)

    @pl.when(at_end)
    def _():
        attend(0)

    project(2)
    finish(2)

    @pl.when(jnp.logical_not(at_end))
    def _():
        attend(0)

    attend(1)

    load_out.wait()
    mix[...] = jnp.dot(comb[z], wo_own[...], preferred_element_type=jnp.float32)

    def collect(step, carry):
        shared_from(step).wait_recv()
        return carry

    lax.fori_loop(1, plane, collect, 0)

    def pass_comb(shard, head):
        @pl.when(z < shard)
        def _():
            comb_hop(0, shard, head).wait_recv()

            @pl.when(z > 0)
            def _():
                comb_hop(0, shard, head).start()

        @pl.when(z > shard)
        def _():
            comb_hop(1, shard, head).wait_recv()

            @pl.when(z < n_head - 1)
            def _():
                comb_hop(1, shard, head).start()

    for low, high in center_out(n_head):
        near = jnp.where(2 * z < n_head, low, high)
        for head in range(heads + 1):
            if head < heads:
                pass_comb(near, head)
            if head and low != high:
                pass_comb(low + high - near, head - 1)

        for shard in (low, high)[: 1 + (low != high)]:

            @pl.when(z != shard)
            def _():
                mix[...] += jnp.dot(
                    comb[shard],
                    wo_far[lax.rem(shard - z - 1 + n_head, n_head)],
                    preferred_element_type=jnp.float32,
                )

    out[...] = mix[...].astype(jnp.bfloat16)

    for step in range(1, n_head):
        fetch(step).wait_send()

    def drain_share(step, carry):
        share(step).wait_send()
        return carry

    lax.fori_loop(1, plane, drain_share, 0)

    def drain_line(shard, carry):
        @pl.when((shard >= z) & (z > 0))
        def _():
            for strand in range(2):
                for part_id in range(PIECES):
                    hop(0, strand, shard, part_id, xbuf).wait_send()
            for head in range(heads):
                comb_hop(0, shard, head).wait_send()

        @pl.when((shard <= z) & (z < n_head - 1))
        def _():
            for strand in range(2):
                for part_id in range(PIECES):
                    hop(1, strand, shard, part_id, xbuf).wait_send()
            for head in range(heads):
                comb_hop(1, shard, head).wait_send()

        return carry

    lax.fori_loop(0, n_head, drain_line, 0)

    def drain_ctx(shard, carry):
        for strand in range(2):

            @pl.when(passes_on[strand] & (shard <= me if strand == 0 else shard >= me))
            def _():
                for head in range(heads):
                    pass_kv(strand, shard, head).wait_send()

        return carry

    lax.fori_loop(0, n_ctx, drain_ctx, 0)
    for step in range(1, n_ctx):

        @pl.when(me >= step)
        def _():
            early_kv(me, step).wait_send()


def anywhere():
    return pl.BlockSpec(memory_space=pl.ANY)


def shards(
    hidden,
    strand_bases,
    variant_sites,
    base_shift,
    base_embed,
    query_weight,
    key_weight,
    value_weight,
    out_weight,
):
    rows, feats = hidden.shape[1], hidden.shape[2]
    n_groups = lax.axis_size("groups")
    n_ctx = lax.axis_size("ctx")
    n_head = lax.axis_size("head")
    slots = 2 * VAR_DEV
    wide = rows + slots
    hw = query_weight.shape[1]
    heads = hw // HEAD_DIM
    width = query_weight.shape[0]
    count = variant_sites.shape[0]
    plane = n_groups * n_ctx

    half = HEAD_DIM // 2
    freq = np.power(np.float32(ROPE_BASE), -np.arange(half, dtype=np.float32) * 2.0 / HEAD_DIM)
    freq = np.concatenate([freq, freq]).astype(np.float32)[None, :]

    f32, bf16, i32 = jnp.float32, jnp.bfloat16, jnp.int32
    dma = pltpu.SemaphoreType.DMA
    return pl.pallas_call(
        functools.partial(fused_kernel, n_groups, n_ctx, n_head),
        out_shape=jax.ShapeDtypeStruct((rows, feats), bf16),
        in_specs=[anywhere()] * 10,
        out_specs=pl.BlockSpec(memory_space=pltpu.VMEM),
        scratch_shapes=[
            pltpu.VMEM((2, n_head, rows, feats), bf16),
            pltpu.VMEM((3, width, hw), bf16),
            pltpu.VMEM((hw, feats), bf16),
            pltpu.VMEM((max(n_head - 1, 1), hw, feats), bf16),
            pltpu.VMEM((1, rows), i32),
            pltpu.VMEM((1, count), i32),
            pltpu.VMEM((1, count), i32),
            pltpu.VMEM((4, width), bf16),
            pltpu.VMEM((1, HEAD_DIM), f32),
            pltpu.VMEM((wide, feats), bf16),
            pltpu.VMEM((wide, 3 * hw), f32),
            pltpu.VMEM((2, slots, width), f32),
            pltpu.VMEM((slots, rows), bf16),
            pltpu.VMEM((rows, slots), bf16),
            pltpu.VMEM((rows, 1), f32),
            pltpu.VMEM((2, n_ctx, 1, wide), f32),
            pltpu.VMEM((2, wide, HEAD_DIM), f32),
            pltpu.VMEM((2, wide, HEAD_DIM), f32),
            pltpu.VMEM((2, 2, heads, rows, HEAD_DIM), bf16),
            pltpu.VMEM((2, n_ctx, heads, wide, 2 * HEAD_DIM), bf16),
            pltpu.VMEM((2, rows, 1), f32),
            pltpu.VMEM((2, rows, 1), f32),
            pltpu.VMEM((2, rows, HEAD_DIM), f32),
            pltpu.VMEM((heads, rows, HEAD_DIM), f32),
            pltpu.VMEM((n_head, rows, hw), bf16),
            pltpu.VMEM((rows, feats), f32),
            dma((5,)),
            dma((2,)),
            dma((4,)),
            dma((2, 2, n_head, PIECES)),
            dma((2, n_head, PIECES)),
            dma((max(n_head - 1, 1),)),
            dma((max(n_head - 1, 1),)),
            dma((plane,)),
            dma((plane,)),
            dma((2, n_ctx, heads)),
            dma((2, n_ctx, heads)),
            dma((max(n_ctx - 1, 1),)),
            dma((max(n_ctx - 1, 1),)),
            dma((2, n_head, heads)),
            dma((n_head, heads)),
        ],
        compiler_params=pltpu.CompilerParams(
            collective_id=0, has_side_effects=True, vmem_limit_bytes=VMEM_LIMIT
        ),
        name="fused",
    )(
        hidden,
        strand_bases[None, :],
        variant_sites[None, :],
        base_shift[None, :],
        base_embed,
        jnp.asarray(freq),
        query_weight,
        key_weight,
        value_weight,
        out_weight,
    )


def solution(mesh):
    return jax.shard_map(
        shards,
        mesh=mesh,
        in_specs=(
            P(None, ("groups", "ctx"), "head"),
            P(("groups", "ctx")),
            P("groups"),
            P("groups"),
            P(),
            P(None, "head"),
            P(None, "head"),
            P(None, "head"),
            P("head", None),
        ),
        out_specs=P(("groups", "ctx"), "head"),
        check_vma=False,
    )
```
